256 devices in a mesh: chan: 64 (over z, y, x_hi), grp: 4 (over x_lo, core).
Axes of the slice: x: 4 (x_hi: 2, x_lo: 2; x = x_hi * 2 + x_lo), y: 4, z: 8, core: 2. Of those that a mesh axis runs over, the one named last changes fastest.
Arguments:
- gate_up: bfloat16 [4096, 2, 28672], P('grp', None, 'chan'), may hold values from -6 to 6
- counts: int32 [4], P('grp'), may hold values from 512 to 1024
- panels: int32 [2, 512], replicated, may hold values from 0 to 28671, as said below
- inverses: float32 [2, 512, 512], replicated
- down_weight: bfloat16 [28672, 8192], P('chan', 'grp'), may hold values from -6 to 6
Outputs:
- pruned_weight: bfloat16 [28672, 8192], P('chan', 'grp')
The draws below stay inside these ranges and needn't reach their ends.
Inputs may be any that keep to these rules, and one draw needn't show every extreme that they name: `panels`: the entries 512 // 64 * s to 512 // 64 * (s + 1) - 1 of each panel lie in channels s * (28672 // 64) to (s + 1) * (28672 // 64) - 1; all 1024 indices are different.
All inputs are finite; a program needn't handle non-finite values.
Results may differ from the reference program's by a relative error of at most 0.0051.
Values may be sent and summed in bfloat16 or wider, within the bound.
No kernel may reach another device: no remote copies, remote signals or barrier semaphores. Data moves between devices by JAX's collectives and lax.ppermute only.
A program may use at most 64 MiB of HBM per device.

```python
import math
import jax
import jax.numpy as jnp
from jax import lax

D = 8192
FF = 28672
PANEL = 512
TOK_DEV = 1024
TOKENS = 4096
N_CHAN = 64
N_GRP = 4


def draw_panels(key, part):
    local = FF // N_CHAN
    share = PANEL // N_CHAN
    keys = jax.random.split(key, N_CHAN)

    def choose(single):
        return jax.random.permutation(single, local)[:2 * share].astype(jnp.int32)
    picks = jax.vmap(choose)(keys)
    picks = picks + (jnp.arange(N_CHAN, dtype=jnp.int32) * local)[:, None]
    first_panel = picks[:, :share].reshape(-1)
    second_panel = picks[:, share:].reshape(-1)
    return jnp.stack([first_panel, second_panel]).astype(jnp.int32)


def draw_inverses(key, part):
    key_diag = jax.random.fold_in(key, 11)
    key_off = jax.random.fold_in(key, 12)
    diagonal = jax.random.uniform(key_diag, (2, PANEL), jnp.float32, 2.0, 6.0)
    off = jax.random.normal(key_off, (2, PANEL, PANEL), jnp.float32) * (1.5 / math.sqrt(PANEL))
    off = (off + jnp.swapaxes(off, 1, 2)) / math.sqrt(2.0)
    return (off + diagonal[:, :, None] * jnp.eye(PANEL, dtype=jnp.float32)[None]).astype(jnp.float32)


def plant(drawn, key, low, largest):
    longest = drawn.shape.index(max(drawn.shape))
    spots = []
    for shift in (0, 1):
        where = [jax.random.randint(jax.random.fold_in(key, axis), (), 0, length) for axis, length in enumerate(drawn.shape)]
        where[longest] = (where[longest] + shift) % drawn.shape[longest]
        spots.append(tuple(where))
    return drawn.at[spots[0]].set(low).at[spots[1]].set(largest)


def block_scale(rng, extent, shards, least, high):
    def one(position, blocks):
        heights = jax.random.uniform(jax.random.fold_in(jax.random.fold_in(rng, 6), position), (blocks,), jnp.float32, least / len(shards), high / len(shards))
        return jnp.repeat(jnp.exp(heights), extent[position] // blocks).reshape((-1,) + (1,) * (len(extent) - position - 1))

    gain = one(*shards[0])
    for cut in shards[1:]:
        gain = gain * one(*cut)
    return gain


def normal_values(key, extent, width, reach, cuts=(), kind=jnp.bfloat16):
    result = width * jax.random.normal(key, extent, jnp.float32)
    if cuts:
        result = result * block_scale(key, extent, cuts, -0.22, 0.18)
    return jnp.clip(result, -reach, reach).astype(kind)


def setup_inputs(seed: int = 0) -> dict:
    splits = jax.random.split(jax.random.key(seed), 6)
    return {
        "gate_up": normal_values(splits[0], (TOKENS, 2, FF), 1.0, 6.0, ((0, 4), (2, 64))),
        "counts": plant(jax.random.randint(splits[1], (N_GRP,), TOK_DEV // 2, TOK_DEV + 1), jax.random.fold_in(splits[1], 1), TOK_DEV // 2, TOK_DEV).astype(jnp.int32),
        "panels": draw_panels(jax.random.fold_in(splits[5], 71), 0),
        "inverses": draw_inverses(jax.random.fold_in(splits[5], 71), 0),
        "down_weight": normal_values(splits[4], (FF, D), 1.0, 6.0, ((0, 64), (1, 4))),
    }


def reference(gate_up, counts, panels, inverses, down_weight):
    slot = jnp.arange(TOKENS, dtype=jnp.int32)
    valid = (slot % TOK_DEV < jnp.repeat(counts, TOK_DEV)).astype(jnp.float32)
    total = jnp.sum(counts.astype(jnp.float32))
    gate_half = gate_up[:, 0, :].astype(jnp.float32)
    up_half = gate_up[:, 1, :].astype(jnp.float32)
    hidden = (jax.nn.silu(gate_half) * up_half * valid[:, None]).astype(jnp.bfloat16)
    weight = down_weight.astype(jnp.float32)
    for panel_no in range(2):
        picked = panels[panel_no]
        columns = jnp.take(hidden, picked, axis=1)
        hess = lax.dot_general(hidden, columns, (((0,), (0,)), ((), ())), preferred_element_type=jnp.float32) / total
        update = jnp.dot(inverses[panel_no], jnp.take(weight, picked, axis=0), precision=lax.Precision.HIGHEST)
        weight = weight - jnp.dot(hess, update, precision=lax.Precision.HIGHEST)
        removed = panels[:panel_no + 1].reshape(-1).astype(jnp.int32)
        weight = weight.at[removed].set(0.0)
    return weight.astype(jnp.bfloat16)
```

```python
import jax
import jax.numpy as jnp
import numpy as np
from jax import lax
from jax.sharding import Mesh, PartitionSpec as P

SIZES = {"z": 8, "y": 4, "x": 2}
NAMES = {"z": "z", "y": "y", "x": "xh"}
ACT_CUTS = (("zxy", 384), ("zyx", 384), ("yxz", 256))
ROW_CUTS = (("zxy", 896), ("zyx", 768), ("yxz", 384))
BF16 = jnp.bfloat16


def shift(x, axis, by):
    n = lax.axis_size(axis)
    return lax.ppermute(x, axis, [(i, (i + by) % n) for i in range(n)])


def neighbours(x, letter):
    axis = NAMES[letter]
    return jnp.stack([x] + [shift(x, axis, k) for k in range(1, SIZES[letter])])


def gather_cut(x, order):
    for letter in order:
        x = neighbours(x, letter)
    dims = list(reversed(order))
    want = [dims.index(c) for c in "yxz"]
    return jnp.transpose(x, (*want, 3, 4))


def gather_all(x, cuts):
    at, done = 0, []
    for order, width in cuts:
        piece = gather_cut(lax.slice_in_dim(x, at, at + width, axis=1), order)
        piece = piece.reshape(64, 2, 8, width).transpose(1, 0, 2, 3).reshape(1024, width)
        done.append(piece)
        at += width
    return done


def order_of_channels(share):
    back = np.stack(np.meshgrid(np.arange(4), np.arange(2), np.arange(8), indexing="ij"), -1).reshape(-1, 3)
    y = (lax.axis_index("y") - back[:, 0]) % 4
    x = (lax.axis_index("xh") - back[:, 1]) % 2
    z = (lax.axis_index("z") - back[:, 2]) % 8
    chip = z * 8 + y * 2 + x
    return (chip[:, None] * share + np.arange(share)[None, :]).reshape(-1)


def body(gate_up, counts, panels, inverses, down_weight):
    local = gate_up.shape[2]
    panel = panels.shape[1]
    share = panel // 64
    shard = lax.axis_index("z") * 8 + lax.axis_index("y") * 2 + lax.axis_index("xh")
    core = lax.axis_index("co")
    high = lax.Precision.HIGHEST
    mine = lax.dynamic_slice(panels, (0, shard * share), (2, share)).reshape(-1) - shard * local
    onehot = mine[:, None] == jnp.arange(local, dtype=jnp.int32)[None, :]
    select = onehot.astype(BF16)

    slot = jnp.arange(gate_up.shape[0], dtype=jnp.int32)
    valid = (slot < counts[0]).astype(jnp.float32)
    gate = gate_up[:, 0, :].astype(jnp.float32)
    up = gate_up[:, 1, :].astype(jnp.float32)
    hidden = (jax.nn.silu(gate) * up * valid[:, None]).astype(BF16)
    acts = lax.dot_general(select, hidden, (((1,), (1,)), ((), ())), preferred_element_type=jnp.float32).astype(BF16)
    rows = jnp.dot(select, down_weight, preferred_element_type=jnp.float32).astype(BF16)

    acts_all = jnp.concatenate(gather_all(acts, ACT_CUTS), axis=1)
    rows_all = gather_all(rows, ROW_CUTS)

    total = counts
    total = total + shift(total, "co", 1)
    total = total + shift(total, "xl", 1)
    scale = 1.0 / total[0].astype(jnp.float32)

    place = order_of_channels(share)
    turn = (place[:, None] == jnp.arange(panel, dtype=jnp.int32)[None, :]).astype(jnp.float32)
    inv = [
        jnp.dot(jnp.dot(turn, inverses[j], precision=high), turn.T, precision=high) for j in range(2)
    ]

    hidden_t = hidden.T
    nt = (((1,), (1,)), ((), ()))
    first_acts, second_acts = acts_all[:panel], acts_all[panel:]
    left = jnp.concatenate([hidden_t, second_acts], axis=0)
    first = lax.dot_general(left, first_acts, nt, preferred_element_type=jnp.float32)
    second = lax.dot_general(hidden_t, second_acts, nt, preferred_element_type=jnp.float32)
    half, cross_half = local // 2, panel // 2
    parts = jnp.stack(
        [
            jnp.concatenate(
                [
                    first[k * half : (k + 1) * half],
                    second[k * half : (k + 1) * half],
                    first[local + k * cross_half : local + (k + 1) * cross_half],
                ],
                axis=0,
            )
            for k in range(2)
        ]
    )
    zero = core == 0
    keep = jnp.where(zero, parts[0], parts[1])
    give = jnp.where(zero, parts[1], parts[0])
    keep = keep + shift(give.astype(BF16), "co", 1).astype(jnp.float32)
    keep = keep + shift(keep.astype(BF16), "xl", 1).astype(jnp.float32)
    keep = keep * scale
    other = shift(keep.astype(BF16), "co", 1).astype(jnp.float32)
    low, top = jnp.where(zero, keep, other), jnp.where(zero, other, keep)
    first_hess = jnp.concatenate([low[:half], top[:half]], axis=0)
    second_hess = jnp.concatenate([low[half : 2 * half], top[half : 2 * half]], axis=0)
    cross = jnp.concatenate([low[2 * half :], top[2 * half :]], axis=0)

    mid = lax.Precision.HIGH
    second_gain = jnp.dot(second_hess, inv[1], precision=mid)
    first_gain = jnp.dot(first_hess - jnp.dot(second_gain, cross, precision=mid), inv[0], precision=mid)
    gain = jnp.concatenate([first_gain, second_gain], axis=1).astype(BF16)

    gone = jnp.any(onehot, axis=0)[:, None]
    at, outs = 0, []
    for piece in rows_all:
        width = piece.shape[1]
        old = lax.slice_in_dim(down_weight, at, at + width, axis=1).astype(jnp.float32)
        new = old - jnp.dot(gain, piece, preferred_element_type=jnp.float32)
        outs.append(jnp.where(gone, 0.0, new).astype(BF16))
        at += width
    return jnp.concatenate(outs, axis=1)


def solution(mesh):
    fine = Mesh(mesh.devices.reshape(8, 4, 2, 2, 2), ("z", "y", "xh", "xl", "co"))
    chan, grp = ("z", "y", "xh"), ("xl", "co")
    in_specs = (P(grp, None, chan), P(grp), P(), P(), P(chan, grp))
    return jax.shard_map(body, mesh=fine, in_specs=in_specs, out_specs=P(chan, grp), check_vma=False)
```

```python
import jax
import jax.numpy as jnp
from jax import lax
from jax.sharding import Mesh, PartitionSpec as P

BF16 = jnp.bfloat16
F32 = jnp.float32
NT = (((1,), (1,)), ((), ()))


def shift(x, axis, by):
    n = lax.axis_size(axis)
    return lax.ppermute(x, axis, [(i, (i + by) % n) for i in range(n)])


def to_all(x, axes):
    n = lax.axis_size(axes)
    return lax.all_to_all(jnp.broadcast_to(x, (n, *x.shape)), axes, split_axis=0, concat_axis=0, tiled=True)


def place(pieces, axis, dim):
    n, me = lax.axis_size(axis), lax.axis_index(axis)
    shape = list(pieces[0][1].shape)
    shape.insert(dim, n)
    out = jnp.zeros(tuple(shape), pieces[0][1].dtype)
    for back, piece in pieces:
        at = [0] * len(shape)
        at[dim] = (me - back) % n
        out = lax.dynamic_update_slice(out, jnp.expand_dims(piece, dim), at)
    return out


def gather_rows(rows):
    both = place([(0, rows), (1, shift(rows, "xh", 1))], "xh", 1)
    around = place([(0, both)] + [(k, shift(both, "y", k)) for k in (1, 3, 2)], "y", 1)
    return around.reshape(2, 64, rows.shape[-1])


def ring_z(block):
    pieces = [(0, block)]
    ahead, behind = block, block
    for step in (1, 2, 3):
        ahead, behind = shift(ahead, "z", 1), shift(behind, "z", -1)
        pieces += [(step, ahead), (8 - step, behind)]
    half = block.shape[-1] // 2
    far = jnp.concatenate(
        [shift(ahead[..., :half], "z", 1), shift(behind[..., half:], "z", -1)], axis=-1
    )
    pieces.append((4, far))
    return place(pieces, "z", 1).reshape(2, 512, block.shape[-1])


def body(gate_up, counts, panels, inverses, down_weight):
    tokens, _, local = gate_up.shape
    panel = panels.shape[1]
    columns = down_weight.shape[1]
    share = panel // 64
    shard = lax.axis_index("z") * 8 + lax.axis_index("y") * 2 + lax.axis_index("xh")
    zero = lax.axis_index("co") == 0
    mine = lax.dynamic_slice(panels, (0, shard * share), (2, share)).reshape(-1) - shard * local
    onehot = mine[:, None] == jnp.arange(local, dtype=jnp.int32)[None, :]
    select = onehot.astype(BF16)

    rows = jnp.dot(select, down_weight, preferred_element_type=F32).astype(BF16)

    slot = jnp.arange(tokens, dtype=jnp.int32)
    valid = (slot < counts[0]).astype(F32)
    gate = gate_up[:, 0, :].astype(F32)
    up = gate_up[:, 1, :].astype(F32)
    hidden = (jax.nn.silu(gate) * up * valid[:, None]).astype(BF16)
    acts = lax.dot_general(select, hidden, NT, preferred_element_type=F32).astype(BF16)

    acts = to_all(acts, "z").reshape(128, tokens)
    near = gather_rows(rows.reshape(2, share, columns))
    acts = to_all(acts, ("y", "xh"))
    acts = acts.reshape(8, 8, 2, share, tokens).transpose(2, 1, 0, 3, 4).reshape(2, panel, tokens)
    rows_all = ring_z(near).reshape(2 * panel, columns)

    total = counts
    total = total + shift(total, "co", 1)
    total = total + shift(total, "xl", 1)
    scale = 1.0 / total[0].astype(F32)

    left = jnp.concatenate([hidden.T, acts[1]], axis=0)
    first = lax.dot_general(left, acts[0], NT, preferred_element_type=F32)
    second = lax.dot_general(left[:local], acts[1], NT, preferred_element_type=F32)
    half, cross_half = local // 2, panel // 2

    def part(k):
        return jnp.concatenate(
            [
                first[k * half : (k + 1) * half],
                second[k * half : (k + 1) * half],
                first[local + k * cross_half : local + (k + 1) * cross_half],
            ],
            axis=0,
        )

    keep = jnp.where(zero, part(0), part(1))
    give = jnp.where(zero, part(1), part(0)).astype(BF16)
    keep = keep + shift(give, "co", 1).astype(F32)
    keep = keep + shift(keep.astype(BF16), "xl", 1).astype(F32)
    keep = keep * scale
    other = shift(keep.astype(BF16), "co", 1).astype(F32)
    low, top = jnp.where(zero, keep, other), jnp.where(zero, other, keep)
    first_hess = jnp.concatenate([low[:half], top[:half]], axis=0)
    second_hess = jnp.concatenate([low[half : 2 * half], top[half : 2 * half]], axis=0)
    cross = jnp.concatenate([low[2 * half :], top[2 * half :]], axis=0)

    mid = lax.Precision.HIGH
    second_gain = jnp.dot(second_hess, inverses[1], precision=mid)
    first_gain = jnp.dot(first_hess - jnp.dot(second_gain, cross, precision=mid), inverses[0], precision=mid)
    gain = jnp.concatenate([first_gain, second_gain], axis=1).astype(BF16)

    gone = jnp.any(onehot, axis=0)[:, None]
    new = down_weight.astype(F32) - jnp.dot(gain, rows_all, preferred_element_type=F32)
    return jnp.where(gone, 0.0, new).astype(BF16)


def solution(mesh):
    fine = Mesh(mesh.devices.reshape(8, 4, 2, 2, 2), ("z", "y", "xh", "xl", "co"))
    chan, grp = ("z", "y", "xh"), ("xl", "co")
    in_specs = (P(grp, None, chan), P(grp), P(), P(), P(chan, grp))
    return jax.shard_map(body, mesh=fine, in_specs=in_specs, out_specs=P(chan, grp), check_vma=False)
```

```python
import jax
import jax.numpy as jnp
from jax import lax
from jax.sharding import Mesh, PartitionSpec as P


BF16 = jnp.bfloat16
F32 = jnp.float32
NT = (((1,), (1,)), ((), ()))


def shift(x, axis, by):
    n = lax.axis_size(axis)
    return lax.ppermute(x, axis, [(i, (i + by) % n) for i in range(n)])


def to_all(x, axes):
    n = lax.axis_size(axes)
    return lax.all_to_all(jnp.broadcast_to(x, (n, *x.shape)), axes, split_axis=0, concat_axis=0, tiled=True)


def place(pieces, axis, dim):
    n, me = lax.axis_size(axis), lax.axis_index(axis)
    shape = list(pieces[0][1].shape)
    shape.insert(dim, n)
    out = jnp.zeros(tuple(shape), pieces[0][1].dtype)
    for back, piece in pieces:
        at = [0] * len(shape)
        at[dim] = (me - back) % n
        out = lax.dynamic_update_slice(out, jnp.expand_dims(piece, dim), at)
    return out


def gather_rows(rows):
    other = shift(rows, "xh", 1)
    both = place([(0, rows), (1, other)], "xh", 1)
    others = [(k, shift(both, "y", k)) for k in (1, 3, 2)]
    around = place([(0, both)] + others, "y", 1)
    return around.reshape(2, 64, rows.shape[-1])


def ring_z(block):
    pieces = [(0, block)]
    ahead, behind = block, block
    for step in (1, 2, 3):
        ahead, behind = shift(ahead, "z", 1), shift(behind, "z", -1)
        pieces += [(step, ahead), (8 - step, behind)]
    half = block.shape[-1] // 2
    ahead, behind = ahead[..., :half], behind[..., half:]
    ahead, behind = shift(ahead, "z", 1), shift(behind, "z", -1)
    far = jnp.concatenate([ahead, behind], axis=-1)
    pieces.append((4, far))
    return place(pieces, "z", 1).reshape(2, 512, block.shape[-1])


def compute(gate_up, counts, panels, inverses, down_weight):
    tokens, _, local = gate_up.shape
    panel = panels.shape[1]
    columns = down_weight.shape[1]
    share = panel // 64
    shard = lax.axis_index("z") * 8 + lax.axis_index("y") * 2 + lax.axis_index("xh")
    zero = lax.axis_index("co") == 0
    mine = lax.dynamic_slice(panels, (0, shard * share), (2, share)).reshape(-1) - shard * local
    onehot = mine[:, None] == jnp.arange(local, dtype=jnp.int32)[None, :]
    select = onehot.astype(BF16)

    rows = jnp.dot(select, down_weight, preferred_element_type=F32).astype(BF16)

    slot = jnp.arange(tokens, dtype=jnp.int32)
    valid = (slot < counts[0]).astype(F32)
    gate = gate_up[:, 0, :].astype(F32)
    up = gate_up[:, 1, :].astype(F32)
    hidden = (jax.nn.silu(gate) * up * valid[:, None]).astype(BF16)
    acts = lax.dot_general(select, hidden, NT, preferred_element_type=F32).astype(BF16)

    acts = to_all(acts, "z").reshape(128, tokens)
    near = gather_rows(rows.reshape(2, share, columns))
    acts = to_all(acts, ("y", "xh"))
    acts = acts.reshape(8, 8, 2, share, tokens).transpose(2, 1, 0, 3, 4).reshape(2, panel, tokens)
    rows_all = ring_z(near).reshape(2 * panel, columns)

    tens = jnp.arange(8, dtype=jnp.int32)[:, None] == 0
    count = jnp.where(tens, counts[0] // 32, counts[0] % 32).astype(F32)
    count = jnp.broadcast_to(count, (8, panel))

    left = jnp.concatenate([hidden.T, acts[1]], axis=0)
    first = lax.dot_general(left, acts[0], NT, preferred_element_type=F32)
    second = lax.dot_general(left[:local], acts[1], NT, preferred_element_type=F32)
    half, cross_half = local // 2, panel // 2

    def part(k):
        return jnp.concatenate(
            [
                first[k * half : (k + 1) * half],
                second[k * half : (k + 1) * half],
                first[local + k * cross_half : local + (k + 1) * cross_half],
                count,
            ],
            axis=0,
        )

    keep = jnp.where(zero, part(0), part(1))
    give = jnp.where(zero, part(1), part(0)).astype(BF16)
    given = shift(give, "co", 1)
    keep = keep + given.astype(F32)
    give = keep.astype(BF16)
    given = shift(give, "xl", 1)
    keep = keep + given.astype(F32)
    rows_in_half = 2 * half + cross_half
    scale = 1.0 / (32.0 * keep[rows_in_half, 0] + keep[rows_in_half + 1, 0])
    keep = keep[:rows_in_half] * scale
    give = keep.astype(BF16)
    given = shift(give, "co", 1)
    other = given.astype(F32)
    low, top = jnp.where(zero, keep, other), jnp.where(zero, other, keep)
    first_hess = jnp.concatenate([low[:half], top[:half]], axis=0)
    second_hess = jnp.concatenate([low[half : 2 * half], top[half : 2 * half]], axis=0)
    cross = jnp.concatenate([low[2 * half :], top[2 * half :]], axis=0)

    mid = lax.Precision.HIGH
    second_gain = jnp.dot(second_hess, inverses[1], precision=mid)
    first_gain = jnp.dot(first_hess - jnp.dot(second_gain, cross, precision=mid), inverses[0], precision=mid)
    gain = jnp.concatenate([first_gain, second_gain], axis=1).astype(BF16)

    gone = jnp.any(onehot, axis=0)[:, None]
    new = down_weight.astype(F32) - jnp.dot(gain, rows_all, preferred_element_type=F32)
    return jnp.where(gone, 0.0, new).astype(BF16)


def solution(mesh):
    fine = Mesh(mesh.devices.reshape(8, 4, 2, 2, 2), ("z", "y", "xh", "xl", "co"))
    chan, grp = ("z", "y", "xh"), ("xl", "co")
    in_specs = (P(grp, None, chan), P(grp), P(), P(), P(chan, grp))
    return jax.shard_map(compute, mesh=fine, in_specs=in_specs, out_specs=P(chan, grp), check_vma=False)
```

```python
import functools

import jax
import jax.numpy as jnp
from jax import lax
from jax.experimental import pallas as pl
from jax.experimental.pallas import tpu as pltpu
from jax.sharding import Mesh, PartitionSpec as P


BF16 = jnp.bfloat16
F32 = jnp.float32
NT = (((1,), (1,)), ((), ()))
VMEM = pl.BlockSpec(memory_space=pltpu.VMEM)
SMEM = pl.BlockSpec(memory_space=pltpu.SMEM)
HBM = pl.BlockSpec(memory_space=pltpu.HBM)


def shift(x, axis, by):
    n = lax.axis_size(axis)
    return lax.ppermute(x, axis, [(i, (i + by) % n) for i in range(n)])


def to_all(x, axes):
    n = lax.axis_size(axes)
    return lax.all_to_all(jnp.broadcast_to(x, (n, *x.shape)), axes, split_axis=0, concat_axis=0, tiled=True)


def place(pieces, axis, dim):
    n, me = lax.axis_size(axis), lax.axis_index(axis)
    shape = list(pieces[0][1].shape)
    shape.insert(dim, n)
    out = jnp.zeros(tuple(shape), pieces[0][1].dtype)
    for back, piece in pieces:
        at = [0] * len(shape)
        at[dim] = (me - back) % n
        out = lax.dynamic_update_slice(out, jnp.expand_dims(piece, dim), at)
    return out


def gather_rows(rows):
    other = shift(rows, "xh", 1)
    both = place([(0, rows), (1, other)], "xh", 1)
    others = [(k, shift(both, "y", k)) for k in (1, 3, 2)]
    around = place([(0, both)] + others, "y", 1)
    return around.reshape(2, 64, rows.shape[-1])


def ring_z(block):
    pieces = [(0, block)]
    ahead, behind = block, block
    for step in (1, 2, 3):
        ahead, behind = shift(ahead, "z", 1), shift(behind, "z", -1)
        pieces += [(step, ahead), (8 - step, behind)]
    half = block.shape[-1] // 2
    ahead, behind = ahead[..., :half], behind[..., half:]
    ahead, behind = shift(ahead, "z", 1), shift(behind, "z", -1)
    return pieces + [(4, ahead), (4, behind)]


def far(x):
    return pltpu.with_memory_space_constraint(x, pltpu.HBM)


def dot(a, b):
    return jnp.dot(a, b, preferred_element_type=F32)


def dot_nt(a, b):
    return lax.dot_general(a, b, NT, preferred_element_type=F32)


def partial_kernel(core_ref, count_ref, hidden_ref, acts_ref, keep_ref, give_ref):
    half, cross = hidden_ref.shape[0] // 2, acts_ref.shape[1] // 2
    core = core_ref[0]
    count = count_ref[0]
    high = lax.broadcasted_iota(jnp.int32, (8, acts_ref.shape[1]), 0) == 0
    counts = jnp.where(high, count // 32, count % 32).astype(F32)
    for mine, ref in ((core, keep_ref), (1 - core, give_ref)):
        hidden = hidden_ref[pl.ds(pl.multiple_of(mine * half, 32), half), :]
        second = acts_ref[1, pl.ds(pl.multiple_of(mine * cross, 32), cross), :]
        ref[pl.ds(0, half), :] = dot_nt(hidden, acts_ref[0]).astype(ref.dtype)
        ref[pl.ds(half, half), :] = dot_nt(hidden, acts_ref[1]).astype(ref.dtype)
        ref[pl.ds(2 * half, cross), :] = dot_nt(second, acts_ref[0]).astype(ref.dtype)
        ref[pl.ds(2 * half + cross, 8), :] = counts.astype(ref.dtype)


def join_kernel(keep_ref, given_ref, out_ref, give_ref):
    rows = out_ref.shape[0]
    counts = keep_ref[pl.ds(rows, 8), :] + given_ref[pl.ds(rows, 8), :].astype(F32)
    scale = 1.0 / (32.0 * counts[0:1, :] + counts[1:2, :])
    joined = (keep_ref[pl.ds(0, rows), :] + given_ref[pl.ds(0, rows), :].astype(F32)) * scale
    out_ref[...] = joined
    give_ref[...] = joined.astype(BF16)


def split(x):
    high = x.astype(BF16)
    return high, (x - high.astype(F32)).astype(BF16)


def dot3(a, b):
    return dot(a[0], b[0]) + (dot(a[0], b[1]) + dot(a[1], b[0]))


def tail_kernel(
    backs, at_ref, keep_ref, given_ref, inv_ref, stay_ref, *refs
):
    pieces, (old_ref, out_ref, inv_buf, rows_ref, old_buf, new_buf, gain_ref, inv_sems, sems, old_sem, new_sems) = (
        refs[: len(backs)], refs[len(backs):]
    )
    zero, z = at_ref[0] == 0, at_ref[1]
    depth, columns = pieces[0].shape[1:]
    panel = inv_ref.shape[1]
    copies = []
    for i, (back, piece) in enumerate(zip(backs, pieces)):
        width = piece.shape[2]
        left = columns - width if i == len(backs) - 1 else 0
        row = pl.multiple_of(lax.rem(z + 8 - back, 8) * depth, depth)
        for p in range(2):
            copies.append(
                pltpu.make_async_copy(
                    piece.at[p],
                    rows_ref.at[p, pl.ds(row, depth), pl.ds(left, width)],
                    sems.at[i, p],
                )
            )
    old_copy = pltpu.make_async_copy(old_ref, old_buf, old_sem)
    inv_copies = [pltpu.make_async_copy(inv_ref.at[p], inv_buf.at[p], inv_sems.at[p]) for p in (1, 0)]
    for copy in inv_copies:
        copy.start()
    for copy in copies:
        copy.start()
    old_copy.start()

    keep, given = keep_ref[...], given_ref[...].astype(F32)
    low, top = jnp.where(zero, keep, given), jnp.where(zero, given, keep)
    half = old_ref.shape[0] // 2
    for copy in inv_copies:
        copy.wait()
    first_inv, second_inv = split(inv_buf[0]), split(inv_buf[1])
    cross = split(jnp.concatenate([low[2 * half :], top[2 * half :]], axis=0))
    for k, part in enumerate((low, top)):
        second = dot3(split(part[half : 2 * half]), second_inv)
        first = dot3(split(part[:half] - dot3(split(second), cross)), first_inv)
        gain_ref[pl.ds(k * half, half), pl.ds(0, panel)] = first.astype(BF16)
        gain_ref[pl.ds(k * half, half), pl.ds(panel, panel)] = second.astype(BF16)

    for copy in copies:
        copy.wait()
    old_copy.wait()
    stay = stay_ref[...] > 0.0
    gain = gain_ref[...]
    chunks = new_sems.shape[0]
    width = columns // chunks
    outs = []
    for c in range(chunks):
        at = pl.ds(c * width, width)
        change = dot(gain[:, :panel], rows_ref[0, :, at]) + dot(gain[:, panel:], rows_ref[1, :, at])
        new = jnp.where(stay, old_buf[:, at].astype(F32) - change, 0.0)
        new_buf[:, at] = new.astype(BF16)
        outs.append(pltpu.make_async_copy(new_buf.at[:, at], out_ref.at[:, at], new_sems.at[c]))
        outs[-1].start()
    for copy in outs:
        copy.wait()


def compute(gate_up, counts, panels, inverses, down_weight):
    tokens, _, local = gate_up.shape
    panel = panels.shape[1]
    columns = down_weight.shape[1]
    share = panel // 64
    shard = lax.axis_index("z") * 8 + lax.axis_index("y") * 2 + lax.axis_index("xh")
    core = lax.axis_index("co").astype(jnp.int32)
    mine = lax.dynamic_slice(panels, (0, shard * share), (2, share)).reshape(-1) - shard * local
    onehot = mine[:, None] == jnp.arange(local, dtype=jnp.int32)[None, :]
    select = onehot.astype(BF16)

    rows = jnp.dot(select, down_weight, preferred_element_type=F32).astype(BF16)

    slot = jnp.arange(tokens, dtype=jnp.int32)
    valid = (slot < counts[0]).astype(F32)
    gate = gate_up[:, 0, :].astype(F32)
    up = gate_up[:, 1, :].astype(F32)
    hidden = (jax.nn.silu(gate) * up * valid[:, None]).astype(BF16)
    acts = lax.dot_general(select, hidden, NT, preferred_element_type=F32).astype(BF16)

    acts = to_all(acts, "z").reshape(128, tokens)
    near = gather_rows(rows.reshape(2, share, columns))
    acts = to_all(acts, ("y", "xh"))
    acts = acts.reshape(8, 8, 2, share, tokens).transpose(2, 1, 0, 3, 4).reshape(2, panel, tokens)
    pieces = ring_z(near)

    half, cross_half = local // 2, panel // 2
    rows_in_half = 2 * half + cross_half
    keep, give = pl.pallas_call(
        partial_kernel,
        out_shape=(
            jax.ShapeDtypeStruct((rows_in_half + 8, panel), F32),
            jax.ShapeDtypeStruct((rows_in_half + 8, panel), BF16),
        ),
        in_specs=[SMEM, SMEM, VMEM, VMEM],
        out_specs=(VMEM, VMEM),
        compiler_params=pltpu.CompilerParams(vmem_limit_bytes=12 * 1024 * 1024),
        name="partial",
    )(core[None], counts, hidden.T, acts)
    given = shift(give, "co", 1)
    keep = keep + given.astype(F32)
    give = keep.astype(BF16)
    given = shift(give, "xl", 1)
    keep, give = pl.pallas_call(
        join_kernel,
        out_shape=(
            jax.ShapeDtypeStruct((rows_in_half, panel), F32),
            jax.ShapeDtypeStruct((rows_in_half, panel), BF16),
        ),
        in_specs=[VMEM, VMEM],
        out_specs=(VMEM, VMEM),
        compiler_params=pltpu.CompilerParams(vmem_limit_bytes=12 * 1024 * 1024),
        name="join",
    )(keep, given)
    given = shift(give, "co", 1)

    stay = jnp.where(jnp.any(onehot, axis=0), 0.0, 1.0).astype(F32)[:, None]
    at = jnp.stack([core, lax.axis_index("z").astype(jnp.int32)])
    backs = [back for back, _ in pieces]
    return pl.pallas_call(
        functools.partial(tail_kernel, backs),
        out_shape=jax.ShapeDtypeStruct((local, columns), BF16),
        in_specs=[SMEM, VMEM, VMEM, HBM, VMEM] + [HBM] * (len(backs) + 1),
        out_specs=HBM,
        scratch_shapes=[
            pltpu.VMEM((2, panel, panel), F32),
            pltpu.VMEM((2, panel, columns), BF16),
            pltpu.VMEM((local, columns), BF16),
            pltpu.VMEM((local, columns), BF16),
            pltpu.VMEM((local, 2 * panel), BF16),
            pltpu.SemaphoreType.DMA((2,)),
            pltpu.SemaphoreType.DMA((len(backs), 2)),
            pltpu.SemaphoreType.DMA(()),
            pltpu.SemaphoreType.DMA((4,)),
        ],
        compiler_params=pltpu.CompilerParams(vmem_limit_bytes=20 * 1024 * 1024),
        name="tail",
    )(at, keep, given, far(inverses), stay, *[far(piece) for _, piece in pieces], far(down_weight))


def solution(mesh):
    fine = Mesh(mesh.devices.reshape(8, 4, 2, 2, 2), ("z", "y", "xh", "xl", "co"))
    chan, grp = ("z", "y", "xh"), ("xl", "co")
    in_specs = (P(grp, None, chan), P(grp), P(), P(), P(chan, grp))
    return jax.shard_map(compute, mesh=fine, in_specs=in_specs, out_specs=P(chan, grp), check_vma=False)
```

```python
import functools

import jax
import jax.numpy as jnp
from jax import lax
from jax.experimental import pallas as pl
from jax.experimental.pallas import tpu as pltpu
from jax.sharding import Mesh, PartitionSpec as P


BF16 = jnp.bfloat16
F32 = jnp.float32
NT = (((1,), (1,)), ((), ()))
VMEM = pl.BlockSpec(memory_space=pltpu.VMEM)
SMEM = pl.BlockSpec(memory_space=pltpu.SMEM)
HBM = pl.BlockSpec(memory_space=pltpu.HBM)


def shift(x, axis, by):
    n = lax.axis_size(axis)
    return lax.ppermute(x, axis, [(i, (i + by) % n) for i in range(n)])


def to_all(x, axes):
    n = lax.axis_size(axes)
    return lax.all_to_all(jnp.broadcast_to(x, (n, *x.shape)), axes, split_axis=0, concat_axis=0, tiled=True)


def place(pieces, axis, dim):
    n, me = lax.axis_size(axis), lax.axis_index(axis)
    shape = list(pieces[0][1].shape)
    shape.insert(dim, n)
    out = jnp.zeros(tuple(shape), pieces[0][1].dtype)
    for back, piece in pieces:
        at = [0] * len(shape)
        at[dim] = (me - back) % n
        out = lax.dynamic_update_slice(out, jnp.expand_dims(piece, dim), at)
    return out


def gather_rows(rows):
    other = shift(rows, "xh", 1)
    both = place([(0, rows), (1, other)], "xh", 1)
    others = [(k, shift(both, "y", k)) for k in (1, 3, 2)]
    around = place([(0, both)] + others, "y", 1)
    return around.reshape(2, 64, rows.shape[-1])


def spread_acts(block):
    other = shift(block, "xh", 1)
    block = place([(0, block), (1, other)], "xh", 0)
    ahead, behind = shift(block, "y", 1), shift(block, "y", -1)
    left, right = shift(ahead[:1], "y", 1), shift(behind[1:], "y", -1)
    far_block = jnp.concatenate([left, right], axis=0)
    return place([(0, block), (1, ahead), (3, behind), (2, far_block)], "y", 0)


def ring_z(block):
    pieces = [(0, block)]
    ahead, behind = block, block
    for step in (1, 2, 3):
        ahead, behind = shift(ahead, "z", 1), shift(behind, "z", -1)
        pieces += [(step, ahead), (8 - step, behind)]
    half = block.shape[-1] // 2
    ahead, behind = ahead[..., :half], behind[..., half:]
    ahead, behind = shift(ahead, "z", 1), shift(behind, "z", -1)
    return pieces + [(4, ahead), (4, behind)]


def far(x):
    return pltpu.with_memory_space_constraint(x, pltpu.HBM)


def dot(a, b):
    return jnp.dot(a, b, preferred_element_type=F32)


def dot_nt(a, b):
    return lax.dot_general(a, b, NT, preferred_element_type=F32)


def partial_kernel(core_ref, count_ref, hidden_ref, acts_ref, keep_ref, give_ref):
    half, cross = hidden_ref.shape[0] // 2, acts_ref.shape[1] // 2
    core = core_ref[0]
    count = count_ref[0]
    high = lax.broadcasted_iota(jnp.int32, (8, acts_ref.shape[1]), 0) == 0
    counts = jnp.where(high, count // 32, count % 32).astype(F32)
    for mine, ref in ((core, keep_ref), (1 - core, give_ref)):
        hidden = hidden_ref[pl.ds(pl.multiple_of(mine * half, 32), half), :]
        second = acts_ref[1, pl.ds(pl.multiple_of(mine * cross, 32), cross), :]
        ref[pl.ds(0, half), :] = dot_nt(hidden, acts_ref[0]).astype(ref.dtype)
        ref[pl.ds(half, half), :] = dot_nt(hidden, acts_ref[1]).astype(ref.dtype)
        ref[pl.ds(2 * half, cross), :] = dot_nt(second, acts_ref[0]).astype(ref.dtype)
        ref[pl.ds(2 * half + cross, 8), :] = counts.astype(ref.dtype)


def join_kernel(keep_ref, given_ref, out_ref, give_ref):
    rows = out_ref.shape[0]
    counts = keep_ref[pl.ds(rows, 8), :] + given_ref[pl.ds(rows, 8), :].astype(F32)
    scale = 1.0 / (32.0 * counts[0:1, :] + counts[1:2, :])
    joined = (keep_ref[pl.ds(0, rows), :] + given_ref[pl.ds(0, rows), :].astype(F32)) * scale
    out_ref[...] = joined
    give_ref[...] = joined.astype(BF16)


def split(x):
    high = x.astype(BF16)
    return high, (x - high.astype(F32)).astype(BF16)


def dot3(a, b):
    return dot(a[0], b[0]) + (dot(a[0], b[1]) + dot(a[1], b[0]))


def split_kernel(x_ref, high_ref, low_ref):
    high_ref[...], low_ref[...] = split(x_ref[...])


def tail_kernel(backs, at_ref, keep_ref, given_ref, high_ref, low_ref, stay_ref, *refs):
    pieces, (old_ref, out_ref, rows_ref, old_buf, new_buf, sems, old_sem, new_sems) = (
        refs[: len(backs)], refs[len(backs):]
    )
    zero, z = at_ref[0] == 0, at_ref[1]
    depth, columns = pieces[0].shape[1:]
    copies = []
    for i, (back, piece) in enumerate(zip(backs, pieces)):
        width = piece.shape[2]
        left = columns - width if i == len(backs) - 1 else 0
        row = pl.multiple_of(lax.rem(z + 8 - back, 8) * depth, depth)
        for p in range(2):
            copies.append(
                pltpu.make_async_copy(
                    piece.at[p],
                    rows_ref.at[p, pl.ds(row, depth), pl.ds(left, width)],
                    sems.at[i, p],
                )
            )
    old_copy = pltpu.make_async_copy(old_ref, old_buf, old_sem)
    for copy in copies:
        copy.start()
    old_copy.start()

    keep, given = keep_ref[...], given_ref[...].astype(F32)
    low, top = jnp.where(zero, keep, given), jnp.where(zero, given, keep)
    half = old_ref.shape[0] // 2
    first_hess = jnp.concatenate([low[:half], top[:half]], axis=0)
    second_hess = jnp.concatenate([low[half : 2 * half], top[half : 2 * half]], axis=0)
    cross = jnp.concatenate([low[2 * half :], top[2 * half :]], axis=0)
    second = dot3(split(second_hess), (high_ref[1], low_ref[1]))
    first = dot3(split(first_hess - dot3(split(second), split(cross))), (high_ref[0], low_ref[0]))
    first, second = first.astype(BF16), second.astype(BF16)

    for copy in copies:
        copy.wait()
    old_copy.wait()
    stay = stay_ref[...] > 0.0
    chunks = new_sems.shape[0]
    width = columns // chunks
    outs = []
    for c in range(chunks):
        at = pl.ds(c * width, width)
        change = dot(first, rows_ref[0, :, at]) + dot(second, rows_ref[1, :, at])
        new = jnp.where(stay, old_buf[:, at].astype(F32) - change, 0.0)
        new_buf[:, at] = new.astype(BF16)
        outs.append(pltpu.make_async_copy(new_buf.at[:, at], out_ref.at[:, at], new_sems.at[c]))
        outs[-1].start()
    for copy in outs:
        copy.wait()


def compute(gate_up, counts, panels, inverses, down_weight):
    tokens, _, local = gate_up.shape
    panel = panels.shape[1]
    columns = down_weight.shape[1]
    share = panel // 64
    shard = lax.axis_index("z") * 8 + lax.axis_index("y") * 2 + lax.axis_index("xh")
    core = lax.axis_index("co").astype(jnp.int32)
    mine = lax.dynamic_slice(panels, (0, shard * share), (2, share)).reshape(-1) - shard * local
    onehot = mine[:, None] == jnp.arange(local, dtype=jnp.int32)[None, :]
    select = onehot.astype(BF16)

    rows = jnp.dot(select, down_weight, preferred_element_type=F32).astype(BF16)

    slot = jnp.arange(tokens, dtype=jnp.int32)
    valid = (slot < counts[0]).astype(F32)
    gate = gate_up[:, 0, :].astype(F32)
    up = gate_up[:, 1, :].astype(F32)
    hidden = (jax.nn.silu(gate) * up * valid[:, None]).astype(BF16)
    acts = lax.dot_general(select, hidden, NT, preferred_element_type=F32).astype(BF16)

    acts = to_all(acts, "z").reshape(128, tokens)
    near = gather_rows(rows.reshape(2, share, columns))
    acts = spread_acts(acts).reshape(4, 2, 8, 2, share, tokens)
    acts = acts.transpose(3, 2, 0, 1, 4, 5).reshape(2, panel, tokens)
    pieces = ring_z(near)
    inverses, _ = lax.optimization_barrier((inverses, near))
    parts = pl.pallas_call(
        split_kernel,
        out_shape=(jax.ShapeDtypeStruct(inverses.shape, BF16),) * 2,
        in_specs=[VMEM],
        out_specs=(VMEM, VMEM),
        compiler_params=pltpu.CompilerParams(vmem_limit_bytes=12 * 1024 * 1024),
        name="split",
    )(inverses)

    half, cross_half = local // 2, panel // 2
    rows_in_half = 2 * half + cross_half
    keep, give = pl.pallas_call(
        partial_kernel,
        out_shape=(
            jax.ShapeDtypeStruct((rows_in_half + 8, panel), F32),
            jax.ShapeDtypeStruct((rows_in_half + 8, panel), BF16),
        ),
        in_specs=[SMEM, SMEM, VMEM, VMEM],
        out_specs=(VMEM, VMEM),
        compiler_params=pltpu.CompilerParams(vmem_limit_bytes=12 * 1024 * 1024),
        name="partial",
    )(core[None], counts, hidden.T, acts)
    given = shift(give, "co", 1)
    keep = keep + given.astype(F32)
    give = keep.astype(BF16)
    given = shift(give, "xl", 1)
    keep, give = pl.pallas_call(
        join_kernel,
        out_shape=(
            jax.ShapeDtypeStruct((rows_in_half, panel), F32),
            jax.ShapeDtypeStruct((rows_in_half, panel), BF16),
        ),
        in_specs=[VMEM, VMEM],
        out_specs=(VMEM, VMEM),
        compiler_params=pltpu.CompilerParams(vmem_limit_bytes=12 * 1024 * 1024),
        name="join",
    )(keep, given)
    given = shift(give, "co", 1)

    stay = jnp.where(jnp.any(onehot, axis=0), 0.0, 1.0).astype(F32)[:, None]
    at = jnp.stack([core, lax.axis_index("z").astype(jnp.int32)])
    backs = [back for back, _ in pieces]
    return pl.pallas_call(
        functools.partial(tail_kernel, backs),
        out_shape=jax.ShapeDtypeStruct((local, columns), BF16),
        in_specs=[SMEM, VMEM, VMEM, VMEM, VMEM, VMEM] + [HBM] * (len(backs) + 1),
        out_specs=HBM,
        scratch_shapes=[
            pltpu.VMEM((2, panel, columns), BF16),
            pltpu.VMEM((local, columns), BF16),
            pltpu.VMEM((local, columns), BF16),
            pltpu.SemaphoreType.DMA((len(backs), 2)),
            pltpu.SemaphoreType.DMA(()),
            pltpu.SemaphoreType.DMA((4,)),
        ],
        compiler_params=pltpu.CompilerParams(vmem_limit_bytes=20 * 1024 * 1024),
        name="tail",
    )(at, keep, given, *parts, stay, *[far(piece) for _, piece in pieces], far(down_weight))


def solution(mesh):
    fine = Mesh(mesh.devices.reshape(8, 4, 2, 2, 2), ("z", "y", "xh", "xl", "co"))
    chan, grp = ("z", "y", "xh"), ("xl", "co")
    in_specs = (P(grp, None, chan), P(grp), P(), P(), P(chan, grp))
    return jax.shard_map(compute, mesh=fine, in_specs=in_specs, out_specs=P(chan, grp), check_vma=False)
```

```python
import functools

import jax
import jax.numpy as jnp
from jax import lax
from jax.experimental import pallas as pl
from jax.experimental.pallas import tpu as pltpu
from jax.sharding import Mesh, PartitionSpec as P


BF16 = jnp.bfloat16
F32 = jnp.float32
NT = (((1,), (1,)), ((), ()))
VMEM = pl.BlockSpec(memory_space=pltpu.VMEM)
SMEM = pl.BlockSpec(memory_space=pltpu.SMEM)
HBM = pl.BlockSpec(memory_space=pltpu.HBM)


def shift(x, axis, by):
    n = lax.axis_size(axis)
    return lax.ppermute(x, axis, [(i, (i + by) % n) for i in range(n)])


def to_all(x, axes):
    n = lax.axis_size(axes)
    return lax.all_to_all(jnp.broadcast_to(x, (n, *x.shape)), axes, split_axis=0, concat_axis=0, tiled=True)


def place(pieces, axis, dim):
    n, me = lax.axis_size(axis), lax.axis_index(axis)
    shape = list(pieces[0][1].shape)
    shape.insert(dim, n)
    out = jnp.zeros(tuple(shape), pieces[0][1].dtype)
    for back, piece in pieces:
        at = [0] * len(shape)
        at[dim] = (me - back) % n
        out = lax.dynamic_update_slice(out, jnp.expand_dims(piece, dim), at)
    return out


def gather_rows(rows):
    other = shift(rows, "xh", 1)
    both = place([(0, rows), (1, other)], "xh", 1)
    others = [(k, shift(both, "y", k)) for k in (1, 3, 2)]
    around = place([(0, both)] + others, "y", 1)
    return around.reshape(2, 64, rows.shape[-1])


def spread_acts(block):
    other = shift(block, "xh", 1)
    block = place([(0, block), (1, other)], "xh", 0)
    ahead, behind = shift(block, "y", 1), shift(block, "y", -1)
    left, right = shift(ahead[:1], "y", 1), shift(behind[1:], "y", -1)
    far_block = jnp.concatenate([left, right], axis=0)
    return place([(0, block), (1, ahead), (3, behind), (2, far_block)], "y", 0)


def ring_z(block):
    pieces = [(0, block)]
    ahead, behind = block, block
    for step in (1, 2, 3):
        ahead, behind = shift(ahead, "z", 1), shift(behind, "z", -1)
        pieces += [(step, ahead), (8 - step, behind)]
    ahead, behind = shift(ahead[:1], "z", 1), shift(behind[1:], "z", -1)
    return pieces + [(4, ahead), (4, behind)]


def far(x):
    return pltpu.with_memory_space_constraint(x, pltpu.HBM)


def close(x):
    return pltpu.with_memory_space_constraint(x, pltpu.VMEM)


def dot(a, b):
    return jnp.dot(a, b, preferred_element_type=F32)


def dot_nt(a, b):
    return lax.dot_general(a, b, NT, preferred_element_type=F32)


def partial_kernel(core_ref, count_ref, hidden_ref, acts_ref, keep_ref, give_ref):
    half, cross = hidden_ref.shape[0] // 2, acts_ref.shape[1] // 2
    core = core_ref[0]
    count = count_ref[0]
    high = lax.broadcasted_iota(jnp.int32, (8, acts_ref.shape[1]), 0) == 0
    counts = jnp.where(high, count // 32, count % 32).astype(F32)
    for mine, ref in ((core, keep_ref), (1 - core, give_ref)):
        hidden = hidden_ref[pl.ds(pl.multiple_of(mine * half, 32), half), :]
        second = acts_ref[1, pl.ds(pl.multiple_of(mine * cross, 32), cross), :]
        ref[pl.ds(0, half), :] = dot_nt(hidden, acts_ref[0]).astype(ref.dtype)
        ref[pl.ds(half, half), :] = dot_nt(hidden, acts_ref[1]).astype(ref.dtype)
        ref[pl.ds(2 * half, cross), :] = dot_nt(second, acts_ref[0]).astype(ref.dtype)
        ref[pl.ds(2 * half + cross, 8), :] = counts.astype(ref.dtype)


def cut_kernel(y_ref, keep_ref, given_ref, hess_ref, hess_give, cross_ref, cross_give):
    rows, quarter = hess_ref.shape[0], cross_ref.shape[0] - 8
    at = pl.multiple_of(rows + y_ref[0] * quarter, 64)
    spots = ((hess_ref, hess_give, 0, 0, rows), (cross_ref, cross_give, 0, at, quarter),
             (cross_ref, cross_give, quarter, rows + 4 * quarter, 8))
    for ref, give, to, start, size in spots:
        total = keep_ref[pl.ds(start, size), :] + given_ref[pl.ds(start, size), :].astype(F32)
        ref[pl.ds(to, size), :] = total
        give[pl.ds(to, size), :] = total.astype(BF16)


def join_cross_kernel(keep_ref, given_ref, out_ref, scale_ref):
    total = keep_ref[...] + given_ref[...].astype(F32)
    rows = out_ref.shape[0]
    scale = 1.0 / (32.0 * total[rows : rows + 1] + total[rows + 1 : rows + 2])
    out_ref[...] = (total[:rows] * scale).astype(BF16)
    scale_ref[...] = jnp.broadcast_to(scale, scale_ref.shape)


def join_kernel(backs, y_ref, keep_ref, given_ref, scale_ref, *refs):
    out_ref, rows = refs[-1], keep_ref.shape[0]
    total = keep_ref[...] + given_ref[...].astype(F32)
    out_ref[pl.ds(0, rows), :] = (total * scale_ref[0:1, :]).astype(BF16)
    for back, ref in zip(backs, refs[:-1]):
        quarter = ref.shape[0]
        at = rows + lax.rem(y_ref[0] + 4 - back, 4) * quarter
        out_ref[pl.ds(pl.multiple_of(at, 64), quarter), :] = ref[...]


def split(x):
    high = x.astype(BF16)
    return high, (x - high.astype(F32)).astype(BF16)


def split_kernel(x_ref, high_ref, low_ref):
    high_ref[...], low_ref[...] = split(x_ref[...])


def tail_kernel(backs, at_ref, keep_ref, given_ref, high_ref, low_ref, stay_ref, *refs):
    pieces, (old_ref, out_ref, rows_ref, old_buf, new_buf, sems, old_sem, new_sems) = (
        refs[: len(backs)], refs[len(backs):]
    )
    zero, z = at_ref[0] == 0, at_ref[1]
    depth, columns = pieces[0].shape[1:]
    copies = []
    for i, (back, piece) in enumerate(zip(backs, pieces)):
        row = pl.multiple_of(lax.rem(z + 8 - back, 8) * depth, depth)
        first = 1 if i == len(backs) - 1 else 0
        for p in range(piece.shape[0]):
            copies.append(
                pltpu.make_async_copy(
                    piece.at[p], rows_ref.at[first + p, pl.ds(row, depth), :], sems.at[i, p]
                )
            )
    old_copy = pltpu.make_async_copy(old_ref, old_buf, old_sem)
    for copy in copies:
        copy.start()
    old_copy.start()

    keep, given = keep_ref[...], given_ref[...]
    low, top = jnp.where(zero, keep, given), jnp.where(zero, given, keep)
    half = old_ref.shape[0] // 2
    first_hess = jnp.concatenate([low[:half], top[:half]], axis=0).astype(F32)
    second_hess = jnp.concatenate([low[half : 2 * half], top[half : 2 * half]], axis=0)
    cross = jnp.concatenate([low[2 * half :], top[2 * half :]], axis=0)
    second = (dot(second_hess, high_ref[1]) + dot(second_hess, low_ref[1])).astype(BF16)
    high, rest = split(first_hess - dot(second, cross))
    first = dot(high, high_ref[0]) + (dot(high, low_ref[0]) + dot(rest, high_ref[0]))
    first = first.astype(BF16)

    for copy in copies:
        copy.wait()
    old_copy.wait()
    stay = stay_ref[...] > 0.0
    chunks = new_sems.shape[0]
    width = columns // chunks
    outs = []
    for c in range(chunks):
        at = pl.ds(c * width, width)
        change = dot(first, rows_ref[0, :, at]) + dot(second, rows_ref[1, :, at])
        new = jnp.where(stay, old_buf[:, at].astype(F32) - change, 0.0)
        new_buf[:, at] = new.astype(BF16)
        outs.append(pltpu.make_async_copy(new_buf.at[:, at], out_ref.at[:, at], new_sems.at[c]))
        outs[-1].start()
    for copy in outs:
        copy.wait()


def compute(gate_up, counts, panels, inverses, down_weight):
    tokens, _, local = gate_up.shape
    panel = panels.shape[1]
    columns = down_weight.shape[1]
    share = panel // 64
    shard = lax.axis_index("z") * 8 + lax.axis_index("y") * 2 + lax.axis_index("xh")
    core = lax.axis_index("co").astype(jnp.int32)
    mine = lax.dynamic_slice(panels, (0, shard * share), (2, share)).reshape(-1) - shard * local
    onehot = mine[:, None] == jnp.arange(local, dtype=jnp.int32)[None, :]
    select = onehot.astype(BF16)

    slot = jnp.arange(tokens, dtype=jnp.int32)
    valid = (slot < counts[0]).astype(F32)
    gate = gate_up[:, 0, :].astype(F32)
    up = gate_up[:, 1, :].astype(F32)
    hidden = (jax.nn.silu(gate) * up * valid[:, None]).astype(BF16)
    acts = lax.dot_general(select, hidden, NT, preferred_element_type=F32).astype(BF16)
    acts, select = lax.optimization_barrier((acts, select))
    rows = jnp.dot(select, down_weight, preferred_element_type=F32).astype(BF16)

    acts = to_all(acts, "z").reshape(128, tokens)
    near = gather_rows(rows.reshape(2, share, columns))
    acts = spread_acts(acts).reshape(4, 2, 8, 2, share, tokens)
    acts = acts.transpose(3, 2, 0, 1, 4, 5).reshape(2, panel, tokens)
    pieces = ring_z(near)
    inverses, _ = lax.optimization_barrier((inverses, near))
    parts = pl.pallas_call(
        split_kernel,
        out_shape=(jax.ShapeDtypeStruct(inverses.shape, BF16),) * 2,
        in_specs=[VMEM],
        out_specs=(VMEM, VMEM),
        compiler_params=pltpu.CompilerParams(vmem_limit_bytes=12 * 1024 * 1024),
        name="split",
    )(inverses)

    half, cross_half = local // 2, panel // 2
    rows_in_half = 2 * half + cross_half
    keep, give = pl.pallas_call(
        partial_kernel,
        out_shape=(
            jax.ShapeDtypeStruct((rows_in_half + 8, panel), F32),
            jax.ShapeDtypeStruct((rows_in_half + 8, panel), BF16),
        ),
        in_specs=[SMEM, SMEM, VMEM, VMEM],
        out_specs=(VMEM, VMEM),
        compiler_params=pltpu.CompilerParams(vmem_limit_bytes=12 * 1024 * 1024),
        name="partial",
    )(core[None], counts, hidden.T, acts)
    given = shift(give, "co", 1)
    y = lax.axis_index("y").astype(jnp.int32)[None]
    small = pltpu.CompilerParams(vmem_limit_bytes=8 * 1024 * 1024)
    quarter = cross_half // 4
    hess, hess_give, cross, cross_give = pl.pallas_call(
        cut_kernel,
        out_shape=tuple(
            jax.ShapeDtypeStruct((n, panel), d) for n in (2 * half, quarter + 8) for d in (F32, BF16)
        ),
        in_specs=[SMEM, VMEM, VMEM],
        out_specs=(VMEM,) * 4,
        compiler_params=small,
        name="cut",
    )(y, keep, given)
    cross_given = shift(cross_give, "xl", 1)
    hess_given = shift(hess_give, "xl", 1)
    cross, scale = pl.pallas_call(
        join_cross_kernel,
        out_shape=(jax.ShapeDtypeStruct((quarter, panel), BF16), jax.ShapeDtypeStruct((8, panel), F32)),
        in_specs=[VMEM, VMEM],
        out_specs=(VMEM, VMEM),
        compiler_params=small,
        name="join_cross",
    )(cross, cross_given)
    quarters = [(0, cross)] + [(k, shift(cross, "y", k)) for k in (1, 3, 2)]
    keep = pl.pallas_call(
        functools.partial(join_kernel, [k for k, _ in quarters]),
        out_shape=jax.ShapeDtypeStruct((rows_in_half, panel), BF16),
        in_specs=[SMEM] + [VMEM] * 7,
        out_specs=VMEM,
        compiler_params=small,
        name="join",
    )(y, hess, hess_given, scale, *[piece for _, piece in quarters])
    keep = close(keep)
    given = close(shift(keep, "co", 1))

    stay = jnp.where(jnp.any(onehot, axis=0), 0.0, 1.0).astype(F32)[:, None]
    at = jnp.stack([core, lax.axis_index("z").astype(jnp.int32)])
    backs = [back for back, _ in pieces]
    return pl.pallas_call(
        functools.partial(tail_kernel, backs),
        out_shape=jax.ShapeDtypeStruct((local, columns), BF16),
        in_specs=[SMEM, VMEM, VMEM, VMEM, VMEM, VMEM] + [HBM] * (len(backs) + 1),
        out_specs=HBM,
        scratch_shapes=[
            pltpu.VMEM((2, panel, columns), BF16),
            pltpu.VMEM((local, columns), BF16),
            pltpu.VMEM((local, columns), BF16),
            pltpu.SemaphoreType.DMA((len(backs), 2)),
            pltpu.SemaphoreType.DMA(()),
            pltpu.SemaphoreType.DMA((4,)),
        ],
        compiler_params=pltpu.CompilerParams(vmem_limit_bytes=20 * 1024 * 1024),
        name="tail",
    )(at, keep, given, *parts, stay, *[far(piece) for _, piece in pieces], far(down_weight))


def solution(mesh):
    fine = Mesh(mesh.devices.reshape(8, 4, 2, 2, 2), ("z", "y", "xh", "xl", "co"))
    chan, grp = ("z", "y", "xh"), ("xl", "co")
    in_specs = (P(grp, None, chan), P(grp), P(), P(), P(chan, grp))
    return jax.shard_map(compute, mesh=fine, in_specs=in_specs, out_specs=P(chan, grp), check_vma=False)
```

```python
import functools

import jax
import jax.numpy as jnp
from jax import lax
from jax.experimental import pallas as pl
from jax.experimental.pallas import tpu as pltpu
from jax.sharding import Mesh, PartitionSpec as P


BF16 = jnp.bfloat16
F32 = jnp.float32
NT = (((1,), (1,)), ((), ()))
VMEM = pl.BlockSpec(memory_space=pltpu.VMEM)
SMEM = pl.BlockSpec(memory_space=pltpu.SMEM)
HBM = pl.BlockSpec(memory_space=pltpu.HBM)


def shift(x, axis, by):
    n = lax.axis_size(axis)
    return lax.ppermute(x, axis, [(i, (i + by) % n) for i in range(n)])


def to_all(x, axes):
    n = lax.axis_size(axes)
    return lax.all_to_all(jnp.broadcast_to(x, (n, *x.shape)), axes, split_axis=0, concat_axis=0, tiled=True)


def place(pieces, axis, dim):
    n, me = lax.axis_size(axis), lax.axis_index(axis)
    shape = list(pieces[0][1].shape)
    shape.insert(dim, n)
    out = jnp.zeros(tuple(shape), pieces[0][1].dtype)
    for back, piece in pieces:
        at = [0] * len(shape)
        at[dim] = (me - back) % n
        out = lax.dynamic_update_slice(out, jnp.expand_dims(piece, dim), at)
    return out


def gather_rows(rows):
    other = shift(rows, "xh", 1)
    both = place([(0, rows), (1, other)], "xh", 1)
    others = [(k, shift(both, "y", k)) for k in (1, 3, 2)]
    around = place([(0, both)] + others, "y", 1)
    return around.reshape(2, 64, rows.shape[-1])


def spread_acts(block):
    other = shift(block, "xh", 1)
    block = place([(0, block), (1, other)], "xh", 0)
    ahead, behind = shift(block, "y", 1), shift(block, "y", -1)
    left, right = shift(ahead[:1], "y", 1), shift(behind[1:], "y", -1)
    far_block = jnp.concatenate([left, right], axis=0)
    return place([(0, block), (1, ahead), (3, behind), (2, far_block)], "y", 0)


def ring_z(block):
    pieces = [(0, block)]
    ahead, behind = block, block
    for step in (1, 2, 3):
        ahead, behind = shift(ahead, "z", 1), shift(behind, "z", -1)
        pieces += [(step, ahead), (8 - step, behind)]
    ahead, behind = shift(close(ahead[:1]), "z", 1), shift(close(behind[1:]), "z", -1)
    return pieces + [(4, ahead), (4, behind)]


def close(x):
    return pltpu.with_memory_space_constraint(x, pltpu.VMEM)


def dot(a, b):
    return jnp.dot(a, b, preferred_element_type=F32)


def dot_nt(a, b):
    return lax.dot_general(a, b, NT, preferred_element_type=F32)


def partial_kernel(core_ref, count_ref, hidden_ref, acts_ref, keep_ref, give_ref):
    half, cross = hidden_ref.shape[0] // 2, acts_ref.shape[1] // 2
    core = core_ref[0]
    count = count_ref[0]
    high = lax.broadcasted_iota(jnp.int32, (8, acts_ref.shape[1]), 0) == 0
    counts = jnp.where(high, count // 32, count % 32).astype(F32)
    for mine, ref in ((core, keep_ref), (1 - core, give_ref)):
        hidden = hidden_ref[pl.ds(pl.multiple_of(mine * half, 32), half), :]
        second = acts_ref[1, pl.ds(pl.multiple_of(mine * cross, 32), cross), :]
        ref[pl.ds(0, half), :] = dot_nt(hidden, acts_ref[0]).astype(ref.dtype)
        ref[pl.ds(half, half), :] = dot_nt(hidden, acts_ref[1]).astype(ref.dtype)
        ref[pl.ds(2 * half, cross), :] = dot_nt(second, acts_ref[0]).astype(ref.dtype)
        ref[pl.ds(2 * half + cross, 8), :] = counts.astype(ref.dtype)


def cut_kernel(y_ref, keep_ref, given_ref, hess_ref, hess_give, cross_ref, cross_give):
    rows, quarter = hess_ref.shape[0], cross_ref.shape[0] - 8
    at = pl.multiple_of(rows + y_ref[0] * quarter, 64)
    spots = ((hess_ref, hess_give, 0, 0, rows), (cross_ref, cross_give, 0, at, quarter),
             (cross_ref, cross_give, quarter, rows + 4 * quarter, 8))
    for ref, give, to, start, size in spots:
        total = keep_ref[pl.ds(start, size), :] + given_ref[pl.ds(start, size), :].astype(F32)
        ref[pl.ds(to, size), :] = total
        give[pl.ds(to, size), :] = total.astype(BF16)


def join_cross_kernel(keep_ref, given_ref, out_ref, scale_ref):
    total = keep_ref[...] + given_ref[...].astype(F32)
    rows = out_ref.shape[0]
    scale = 1.0 / (32.0 * total[rows : rows + 1] + total[rows + 1 : rows + 2])
    out_ref[...] = (total[:rows] * scale).astype(BF16)
    scale_ref[...] = jnp.broadcast_to(scale, scale_ref.shape)


def join_kernel(backs, y_ref, keep_ref, given_ref, scale_ref, *refs):
    out_ref, rows = refs[-1], keep_ref.shape[0]
    total = keep_ref[...] + given_ref[...].astype(F32)
    out_ref[pl.ds(0, rows), :] = (total * scale_ref[0:1, :]).astype(BF16)
    for back, ref in zip(backs, refs[:-1]):
        quarter = ref.shape[0]
        at = rows + lax.rem(y_ref[0] + 4 - back, 4) * quarter
        out_ref[pl.ds(pl.multiple_of(at, 64), quarter), :] = ref[...]


def split(x):
    high = x.astype(BF16)
    return high, (x - high.astype(F32)).astype(BF16)


def split_kernel(x_ref, high_ref, low_ref):
    high_ref[...], low_ref[...] = split(x_ref[...])


def tail_kernel(backs, at_ref, keep_ref, given_ref, high_ref, low_ref, stay_ref, old_ref, *refs):
    pieces, (out_ref, rows_ref, new_buf, new_sems) = refs[: len(backs)], refs[len(backs):]
    zero, z = at_ref[0] == 0, at_ref[1]
    depth, columns = pieces[0].shape[1:]

    keep, given = keep_ref[...], given_ref[...]
    low, top = jnp.where(zero, keep, given), jnp.where(zero, given, keep)
    half = old_ref.shape[0] // 2
    first_hess = jnp.concatenate([low[:half], top[:half]], axis=0).astype(F32)
    second_hess = jnp.concatenate([low[half : 2 * half], top[half : 2 * half]], axis=0)
    cross = jnp.concatenate([low[2 * half :], top[2 * half :]], axis=0)
    second = (dot(second_hess, high_ref[1]) + dot(second_hess, low_ref[1])).astype(BF16)
    high, rest = split(first_hess - dot(second, cross))
    first = dot(high, high_ref[0]) + (dot(high, low_ref[0]) + dot(rest, high_ref[0]))
    first = first.astype(BF16)

    for i, (back, piece) in enumerate(zip(backs, pieces)):
        row = pl.multiple_of(lax.rem(z + 8 - back, 8) * depth, depth)
        start = 1 if i == len(backs) - 1 else 0
        for p in range(piece.shape[0]):
            rows_ref[start + p, pl.ds(row, depth), :] = piece[p]
    stay = stay_ref[...] > 0.0
    chunks = new_sems.shape[0]
    width = columns // chunks
    outs = []
    for c in range(chunks):
        at = pl.ds(c * width, width)
        change = dot(first, rows_ref[0, :, at]) + dot(second, rows_ref[1, :, at])
        new = jnp.where(stay, old_ref[:, at].astype(F32) - change, 0.0)
        new_buf[:, at] = new.astype(BF16)
        outs.append(pltpu.make_async_copy(new_buf.at[:, at], out_ref.at[:, at], new_sems.at[c]))
        outs[-1].start()
    for copy in outs:
        copy.wait()


def compute(gate_up, counts, panels, inverses, down_weight):
    tokens, _, local = gate_up.shape
    panel = panels.shape[1]
    columns = down_weight.shape[1]
    share = panel // 64
    shard = lax.axis_index("z") * 8 + lax.axis_index("y") * 2 + lax.axis_index("xh")
    core = lax.axis_index("co").astype(jnp.int32)
    mine = lax.dynamic_slice(panels, (0, shard * share), (2, share)).reshape(-1) - shard * local
    onehot = mine[:, None] == jnp.arange(local, dtype=jnp.int32)[None, :]
    select = onehot.astype(BF16)

    slot = jnp.arange(tokens, dtype=jnp.int32)
    valid = (slot < counts[0]).astype(F32)

    def activate(gate, up):
        return (jax.nn.silu(gate.astype(F32)) * up.astype(F32) * valid).astype(BF16)

    hidden = activate(gate_up[:, 0, :].T, gate_up[:, 1, :].T)
    acts = activate(dot_nt(select, gate_up[:, 0, :]), dot_nt(select, gate_up[:, 1, :]))
    acts, select = lax.optimization_barrier((acts, select))
    rows = jnp.dot(select, down_weight, preferred_element_type=F32).astype(BF16)

    acts = to_all(acts, "z").reshape(128, tokens)
    near = gather_rows(rows.reshape(2, share, columns))
    acts = spread_acts(acts).reshape(4, 2, 8, 2, share, tokens)
    acts = acts.transpose(3, 2, 0, 1, 4, 5).reshape(2, panel, tokens)
    pieces = ring_z(near)
    inverses, _ = lax.optimization_barrier((inverses, near))
    parts = pl.pallas_call(
        split_kernel,
        out_shape=(jax.ShapeDtypeStruct(inverses.shape, BF16),) * 2,
        in_specs=[VMEM],
        out_specs=(VMEM, VMEM),
        compiler_params=pltpu.CompilerParams(vmem_limit_bytes=12 * 1024 * 1024),
        name="split",
    )(inverses)

    half, cross_half = local // 2, panel // 2
    rows_in_half = 2 * half + cross_half
    keep, give = pl.pallas_call(
        partial_kernel,
        out_shape=(
            jax.ShapeDtypeStruct((rows_in_half + 8, panel), F32),
            jax.ShapeDtypeStruct((rows_in_half + 8, panel), BF16),
        ),
        in_specs=[SMEM, SMEM, VMEM, VMEM],
        out_specs=(VMEM, VMEM),
        compiler_params=pltpu.CompilerParams(vmem_limit_bytes=12 * 1024 * 1024),
        name="partial",
    )(core[None], counts, hidden, acts)
    given = shift(give, "co", 1)
    y = lax.axis_index("y").astype(jnp.int32)[None]
    small = pltpu.CompilerParams(vmem_limit_bytes=8 * 1024 * 1024)
    quarter = cross_half // 4
    hess, hess_give, cross, cross_give = pl.pallas_call(
        cut_kernel,
        out_shape=tuple(
            jax.ShapeDtypeStruct((n, panel), d) for n in (2 * half, quarter + 8) for d in (F32, BF16)
        ),
        in_specs=[SMEM, VMEM, VMEM],
        out_specs=(VMEM,) * 4,
        compiler_params=small,
        name="cut",
    )(y, keep, given)
    cross_given = shift(cross_give, "xl", 1)
    hess_given = shift(hess_give, "xl", 1)
    cross, scale = pl.pallas_call(
        join_cross_kernel,
        out_shape=(jax.ShapeDtypeStruct((quarter, panel), BF16), jax.ShapeDtypeStruct((8, panel), F32)),
        in_specs=[VMEM, VMEM],
        out_specs=(VMEM, VMEM),
        compiler_params=small,
        name="join_cross",
    )(cross, cross_given)
    quarters = [(0, cross)] + [(k, shift(cross, "y", k)) for k in (1, 3, 2)]
    keep = pl.pallas_call(
        functools.partial(join_kernel, [k for k, _ in quarters]),
        out_shape=jax.ShapeDtypeStruct((rows_in_half, panel), BF16),
        in_specs=[SMEM] + [VMEM] * 7,
        out_specs=VMEM,
        compiler_params=small,
        name="join",
    )(y, hess, hess_given, scale, *[piece for _, piece in quarters])
    keep = close(keep)
    given = close(shift(keep, "co", 1))

    stay = jnp.where(jnp.any(onehot, axis=0), 0.0, 1.0).astype(F32)[:, None]
    at = jnp.stack([core, lax.axis_index("z").astype(jnp.int32)])
    backs = [back for back, _ in pieces]
    return pl.pallas_call(
        functools.partial(tail_kernel, backs),
        out_shape=jax.ShapeDtypeStruct((local, columns), BF16),
        in_specs=[SMEM] + [VMEM] * (6 + len(backs)),
        out_specs=HBM,
        scratch_shapes=[
            pltpu.VMEM((2, panel, columns), BF16),
            pltpu.VMEM((local, columns), BF16),
            pltpu.SemaphoreType.DMA((4,)),
        ],
        compiler_params=pltpu.CompilerParams(vmem_limit_bytes=16 * 1024 * 1024),
        name="tail",
    )(at, keep, given, *parts, stay, down_weight, *[close(piece) for _, piece in pieces])


def solution(mesh):
    fine = Mesh(mesh.devices.reshape(8, 4, 2, 2, 2), ("z", "y", "xh", "xl", "co"))
    chan, grp = ("z", "y", "xh"), ("xl", "co")
    in_specs = (P(grp, None, chan), P(grp), P(), P(), P(chan, grp))
    return jax.shard_map(compute, mesh=fine, in_specs=in_specs, out_specs=P(chan, grp), check_vma=False)
```

```python
import functools

import jax
import jax.numpy as jnp
from jax import lax
from jax.experimental import pallas as pl
from jax.experimental.pallas import tpu as pltpu
from jax.sharding import Mesh, PartitionSpec as P


BF16 = jnp.bfloat16
F32 = jnp.float32
NT = (((1,), (1,)), ((), ()))
VMEM = pl.BlockSpec(memory_space=pltpu.VMEM)
SMEM = pl.BlockSpec(memory_space=pltpu.SMEM)
HBM = pl.BlockSpec(memory_space=pltpu.HBM)
ANY = pl.BlockSpec(memory_space=pl.ANY)


def shift(x, axis, by):
    n = lax.axis_size(axis)
    return lax.ppermute(x, axis, [(i, (i + by) % n) for i in range(n)])


def to_all(x, axes):
    n = lax.axis_size(axes)
    return lax.all_to_all(jnp.broadcast_to(x, (n, *x.shape)), axes, split_axis=0, concat_axis=0, tiled=True)


def place(pieces, axis, dim):
    n, me = lax.axis_size(axis), lax.axis_index(axis)
    shape = list(pieces[0][1].shape)
    shape.insert(dim, n)
    out = jnp.zeros(tuple(shape), pieces[0][1].dtype)
    for back, piece in pieces:
        at = [0] * len(shape)
        at[dim] = (me - back) % n
        out = lax.dynamic_update_slice(out, jnp.expand_dims(piece, dim), at)
    return out


def gather_rows(rows):
    other = shift(rows, "xh", 1)
    both = place([(0, rows), (1, other)], "xh", 1)
    others = [(k, shift(both, "y", k)) for k in (1, 3, 2)]
    around = place([(0, both)] + others, "y", 1)
    return around.reshape(2, 64, rows.shape[-1])


def spread_acts(block):
    other = shift(block, "xh", 1)
    block = place([(0, block), (1, other)], "xh", 0)
    ahead, behind = shift(block, "y", 1), shift(block, "y", -1)
    left, right = shift(ahead[:1], "y", 1), shift(behind[1:], "y", -1)
    far_block = jnp.concatenate([left, right], axis=0)
    return place([(0, block), (1, ahead), (3, behind), (2, far_block)], "y", 0)


def halve_kernel(ahead_ref, behind_ref, first_ref, second_ref, sems):
    copies = [
        pltpu.make_async_copy(ahead_ref.at[pl.ds(0, 1)], first_ref, sems.at[0]),
        pltpu.make_async_copy(behind_ref.at[pl.ds(1, 1)], second_ref, sems.at[1]),
    ]
    for copy in copies:
        copy.start()
    for copy in copies:
        copy.wait()


def halve(ahead, behind):
    half = jax.ShapeDtypeStruct((1, *ahead.shape[1:]), ahead.dtype)
    return pl.pallas_call(
        halve_kernel,
        out_shape=(half, half),
        in_specs=[ANY, ANY],
        out_specs=(ANY, ANY),
        scratch_shapes=[pltpu.SemaphoreType.DMA((2,))],
        compiler_params=pltpu.CompilerParams(vmem_limit_bytes=2 * 1024 * 1024),
        name="halve",
    )(ahead, behind)


def ring_z(block):
    pieces = [(0, block)]
    ahead, behind = block, block
    for step in (1, 2, 3):
        ahead, behind = shift(ahead, "z", 1), shift(behind, "z", -1)
        pieces += [(step, ahead), (8 - step, behind)]
    ahead, behind = halve(ahead, behind)
    ahead, behind = shift(ahead, "z", 1), shift(behind, "z", -1)
    return pieces + [(4, ahead), (4, behind)]


def far(x):
    return pltpu.with_memory_space_constraint(x, pltpu.HBM)


def close(x):
    return pltpu.with_memory_space_constraint(x, pltpu.VMEM)


def dot(a, b):
    return jnp.dot(a, b, preferred_element_type=F32)


def dot_nt(a, b):
    return lax.dot_general(a, b, NT, preferred_element_type=F32)


def partial_kernel(core_ref, count_ref, hidden_ref, acts_ref, keep_ref, give_ref):
    half, cross = hidden_ref.shape[0] // 2, acts_ref.shape[1] // 2
    core = core_ref[0]
    count = count_ref[0]
    high = lax.broadcasted_iota(jnp.int32, (8, acts_ref.shape[1]), 0) == 0
    counts = jnp.where(high, count // 32, count % 32).astype(F32)
    for mine, ref in ((core, keep_ref), (1 - core, give_ref)):
        hidden = hidden_ref[pl.ds(pl.multiple_of(mine * half, 32), half), :]
        second = acts_ref[1, pl.ds(pl.multiple_of(mine * cross, 32), cross), :]
        ref[pl.ds(0, half), :] = dot_nt(hidden, acts_ref[0]).astype(ref.dtype)
        ref[pl.ds(half, half), :] = dot_nt(hidden, acts_ref[1]).astype(ref.dtype)
        ref[pl.ds(2 * half, cross), :] = dot_nt(second, acts_ref[0]).astype(ref.dtype)
        ref[pl.ds(2 * half + cross, 8), :] = counts.astype(ref.dtype)


def cut_kernel(y_ref, keep_ref, given_ref, hess_ref, hess_give, cross_ref, cross_give):
    rows, quarter = hess_ref.shape[0], cross_ref.shape[0] - 8
    at = pl.multiple_of(rows + y_ref[0] * quarter, 64)
    spots = ((hess_ref, hess_give, 0, 0, rows), (cross_ref, cross_give, 0, at, quarter),
             (cross_ref, cross_give, quarter, rows + 4 * quarter, 8))
    for ref, give, to, start, size in spots:
        total = keep_ref[pl.ds(start, size), :] + given_ref[pl.ds(start, size), :].astype(F32)
        ref[pl.ds(to, size), :] = total
        give[pl.ds(to, size), :] = total.astype(BF16)


def join_cross_kernel(keep_ref, given_ref, out_ref, scale_ref):
    total = keep_ref[...] + given_ref[...].astype(F32)
    rows = out_ref.shape[0]
    scale = 1.0 / (32.0 * total[rows : rows + 1] + total[rows + 1 : rows + 2])
    out_ref[...] = (total[:rows] * scale).astype(BF16)
    scale_ref[...] = jnp.broadcast_to(scale, scale_ref.shape)


def join_kernel(backs, y_ref, keep_ref, given_ref, scale_ref, *refs):
    out_ref, rows = refs[-1], keep_ref.shape[0]
    total = keep_ref[...] + given_ref[...].astype(F32)
    out_ref[pl.ds(0, rows), :] = (total * scale_ref[0:1, :]).astype(BF16)
    for back, ref in zip(backs, refs[:-1]):
        quarter = ref.shape[0]
        at = rows + lax.rem(y_ref[0] + 4 - back, 4) * quarter
        out_ref[pl.ds(pl.multiple_of(at, 64), quarter), :] = ref[...]


def split(x):
    high = x.astype(BF16)
    return high, (x - high.astype(F32)).astype(BF16)


def split_kernel(x_ref, high_ref, low_ref):
    high_ref[...], low_ref[...] = split(x_ref[...])


def tail_kernel(backs, at_ref, keep_ref, given_ref, high_ref, low_ref, stay_ref, *refs):
    pieces, (old_ref, out_ref, rows_ref, old_buf, new_buf, sems, old_sem, new_sems) = (
        refs[: len(backs)], refs[len(backs):]
    )
    zero, z = at_ref[0] == 0, at_ref[1]
    depth, columns = pieces[0].shape[1:]
    chunks = new_sems.shape[0]
    width = columns // chunks
    copies = [[] for _ in range(chunks)]
    for c in range(chunks):
        at = pl.ds(c * width, width)
        for i, (back, piece) in enumerate(zip(backs, pieces)):
            row = pl.multiple_of(lax.rem(z + 8 - back, 8) * depth, depth)
            start = 1 if i == len(backs) - 1 else 0
            for p in range(piece.shape[0]):
                to = rows_ref.at[start + p, pl.ds(row, depth), at]
                copies[c].append(pltpu.make_async_copy(piece.at[p, :, at], to, sems.at[c, i, p]))
        copies[c].append(pltpu.make_async_copy(old_ref.at[:, at], old_buf.at[:, at], old_sem.at[c]))
        for copy in copies[c]:
            copy.start()

    keep, given = keep_ref[...], given_ref[...]
    low, top = jnp.where(zero, keep, given), jnp.where(zero, given, keep)
    half = old_ref.shape[0] // 2
    first_hess = jnp.concatenate([low[:half], top[:half]], axis=0).astype(F32)
    second_hess = jnp.concatenate([low[half : 2 * half], top[half : 2 * half]], axis=0)
    cross = jnp.concatenate([low[2 * half :], top[2 * half :]], axis=0)
    second = (dot(second_hess, high_ref[1]) + dot(second_hess, low_ref[1])).astype(BF16)
    high, rest = split(first_hess - dot(second, cross))
    first = dot(high, high_ref[0]) + (dot(high, low_ref[0]) + dot(rest, high_ref[0]))
    first = first.astype(BF16)

    stay = stay_ref[...] > 0.0
    outs = []
    for c in range(chunks):
        for copy in copies[c]:
            copy.wait()
        at = pl.ds(c * width, width)
        change = dot(first, rows_ref[0, :, at]) + dot(second, rows_ref[1, :, at])
        new = jnp.where(stay, old_buf[:, at].astype(F32) - change, 0.0)
        new_buf[:, at] = new.astype(BF16)
        outs.append(pltpu.make_async_copy(new_buf.at[:, at], out_ref.at[:, at], new_sems.at[c]))
        outs[-1].start()
    for copy in outs:
        copy.wait()


def compute(gate_up, counts, panels, inverses, down_weight):
    tokens, _, local = gate_up.shape
    panel = panels.shape[1]
    columns = down_weight.shape[1]
    share = panel // 64
    shard = lax.axis_index("z") * 8 + lax.axis_index("y") * 2 + lax.axis_index("xh")
    core = lax.axis_index("co").astype(jnp.int32)
    mine = lax.dynamic_slice(panels, (0, shard * share), (2, share)).reshape(-1) - shard * local
    onehot = mine[:, None] == jnp.arange(local, dtype=jnp.int32)[None, :]
    select = onehot.astype(BF16)

    slot = jnp.arange(tokens, dtype=jnp.int32)
    valid = (slot < counts[0]).astype(F32)
    gate = gate_up[:, 0, :].astype(F32)
    up = gate_up[:, 1, :].astype(F32)
    hidden = (jax.nn.silu(gate) * up * valid[:, None]).astype(BF16)
    acts = lax.dot_general(select, hidden, NT, preferred_element_type=F32).astype(BF16)
    acts, select = lax.optimization_barrier((acts, select))
    rows = jnp.dot(select, down_weight, preferred_element_type=F32).astype(BF16)

    acts = to_all(acts, "z").reshape(128, tokens)
    near = gather_rows(rows.reshape(2, share, columns))
    acts = spread_acts(acts).reshape(4, 2, 8, 2, share, tokens)
    acts = acts.transpose(3, 2, 0, 1, 4, 5).reshape(2, panel, tokens)
    pieces = ring_z(near)
    inverses, _ = lax.optimization_barrier((inverses, near))
    parts = pl.pallas_call(
        split_kernel,
        out_shape=(jax.ShapeDtypeStruct(inverses.shape, BF16),) * 2,
        in_specs=[VMEM],
        out_specs=(VMEM, VMEM),
        compiler_params=pltpu.CompilerParams(vmem_limit_bytes=12 * 1024 * 1024),
        name="split",
    )(inverses)

    half, cross_half = local // 2, panel // 2
    rows_in_half = 2 * half + cross_half
    keep, give = pl.pallas_call(
        partial_kernel,
        out_shape=(
            jax.ShapeDtypeStruct((rows_in_half + 8, panel), F32),
            jax.ShapeDtypeStruct((rows_in_half + 8, panel), BF16),
        ),
        in_specs=[SMEM, SMEM, VMEM, VMEM],
        out_specs=(VMEM, VMEM),
        compiler_params=pltpu.CompilerParams(vmem_limit_bytes=12 * 1024 * 1024),
        name="partial",
    )(core[None], counts, hidden.T, acts)
    given = shift(give, "co", 1)
    y = lax.axis_index("y").astype(jnp.int32)[None]
    small = pltpu.CompilerParams(vmem_limit_bytes=8 * 1024 * 1024)
    quarter = cross_half // 4
    hess, hess_give, cross, cross_give = pl.pallas_call(
        cut_kernel,
        out_shape=tuple(
            jax.ShapeDtypeStruct((n, panel), d) for n in (2 * half, quarter + 8) for d in (F32, BF16)
        ),
        in_specs=[SMEM, VMEM, VMEM],
        out_specs=(VMEM,) * 4,
        compiler_params=small,
        name="cut",
    )(y, keep, given)
    cross_given = shift(cross_give, "xl", 1)
    hess_given = shift(hess_give, "xl", 1)
    cross, scale = pl.pallas_call(
        join_cross_kernel,
        out_shape=(jax.ShapeDtypeStruct((quarter, panel), BF16), jax.ShapeDtypeStruct((8, panel), F32)),
        in_specs=[VMEM, VMEM],
        out_specs=(VMEM, VMEM),
        compiler_params=small,
        name="join_cross",
    )(cross, cross_given)
    quarters = [(0, cross)] + [(k, shift(cross, "y", k)) for k in (1, 3, 2)]
    keep = pl.pallas_call(
        functools.partial(join_kernel, [k for k, _ in quarters]),
        out_shape=jax.ShapeDtypeStruct((rows_in_half, panel), BF16),
        in_specs=[SMEM] + [VMEM] * 7,
        out_specs=VMEM,
        compiler_params=small,
        name="join",
    )(y, hess, hess_given, scale, *[piece for _, piece in quarters])
    keep = close(keep)
    given = close(shift(keep, "co", 1))

    stay = jnp.where(jnp.any(onehot, axis=0), 0.0, 1.0).astype(F32)[:, None]
    at = jnp.stack([core, lax.axis_index("z").astype(jnp.int32)])
    backs = [back for back, _ in pieces]
    return pl.pallas_call(
        functools.partial(tail_kernel, backs),
        out_shape=jax.ShapeDtypeStruct((local, columns), BF16),
        in_specs=[SMEM, VMEM, VMEM, VMEM, VMEM, VMEM] + [HBM] * (len(backs) + 1),
        out_specs=HBM,
        scratch_shapes=[
            pltpu.VMEM((2, panel, columns), BF16),
            pltpu.VMEM((local, columns), BF16),
            pltpu.VMEM((local, columns), BF16),
            pltpu.SemaphoreType.DMA((2, len(backs), 2)),
            pltpu.SemaphoreType.DMA((2,)),
            pltpu.SemaphoreType.DMA((2,)),
        ],
        compiler_params=pltpu.CompilerParams(vmem_limit_bytes=20 * 1024 * 1024),
        name="tail",
    )(at, keep, given, *parts, stay, *[far(piece) for _, piece in pieces], far(down_weight))


def solution(mesh):
    fine = Mesh(mesh.devices.reshape(8, 4, 2, 2, 2), ("z", "y", "xh", "xl", "co"))
    chan, grp = ("z", "y", "xh"), ("xl", "co")
    in_specs = (P(grp, None, chan), P(grp), P(), P(), P(chan, grp))
    return jax.shard_map(compute, mesh=fine, in_specs=in_specs, out_specs=P(chan, grp), check_vma=False)
```

```python
import functools

import jax
import jax.numpy as jnp
from jax import lax
from jax.experimental import pallas as pl
from jax.experimental.pallas import tpu as pltpu
from jax.sharding import Mesh, PartitionSpec as P


BF16 = jnp.bfloat16
F32 = jnp.float32
NT = (((1,), (1,)), ((), ()))
VMEM = pl.BlockSpec(memory_space=pltpu.VMEM)
SMEM = pl.BlockSpec(memory_space=pltpu.SMEM)
HBM = pl.BlockSpec(memory_space=pltpu.HBM)
ANY = pl.BlockSpec(memory_space=pl.ANY)


def shift(x, axis, by):
    n = lax.axis_size(axis)
    return lax.ppermute(x, axis, [(i, (i + by) % n) for i in range(n)])


def to_all(x, axes):
    n = lax.axis_size(axes)
    return lax.all_to_all(jnp.broadcast_to(x, (n, *x.shape)), axes, split_axis=0, concat_axis=0, tiled=True)


def place(pieces, axis, dim):
    n, me = lax.axis_size(axis), lax.axis_index(axis)
    shape = list(pieces[0][1].shape)
    shape.insert(dim, n)
    out = jnp.zeros(tuple(shape), pieces[0][1].dtype)
    for back, piece in pieces:
        at = [0] * len(shape)
        at[dim] = (me - back) % n
        out = lax.dynamic_update_slice(out, jnp.expand_dims(piece, dim), at)
    return out


def gather_rows(rows):
    other = shift(rows, "xh", 1)
    both = place([(0, rows), (1, other)], "xh", 1)
    others = [(k, shift(both, "y", k)) for k in (1, 3, 2)]
    around = place([(0, both)] + others, "y", 1)
    return around.reshape(2, 64, rows.shape[-1])


def spread_acts(block):
    other = shift(block, "xh", 1)
    block = place([(0, block), (1, other)], "xh", 0)
    ahead, behind = shift(block, "y", 1), shift(block, "y", -1)
    left, right = shift(ahead[:1], "y", 1), shift(behind[1:], "y", -1)
    far_block = jnp.concatenate([left, right], axis=0)
    return place([(0, block), (1, ahead), (3, behind), (2, far_block)], "y", 0)


def halve_kernel(ahead_ref, behind_ref, first_ref, second_ref, sems):
    copies = [
        pltpu.make_async_copy(ahead_ref.at[pl.ds(0, 1)], first_ref, sems.at[0]),
        pltpu.make_async_copy(behind_ref.at[pl.ds(1, 1)], second_ref, sems.at[1]),
    ]
    for copy in copies:
        copy.start()
    for copy in copies:
        copy.wait()


def halve(ahead, behind):
    half = jax.ShapeDtypeStruct((1, *ahead.shape[1:]), ahead.dtype)
    return pl.pallas_call(
        halve_kernel,
        out_shape=(half, half),
        in_specs=[ANY, ANY],
        out_specs=(ANY, ANY),
        scratch_shapes=[pltpu.SemaphoreType.DMA((2,))],
        compiler_params=pltpu.CompilerParams(vmem_limit_bytes=2 * 1024 * 1024),
        name="halve",
    )(ahead, behind)


def ring_z(block):
    pieces = [(0, block)]
    ahead, behind = block, block
    for step in (1, 2, 3):
        ahead, behind = shift(ahead, "z", 1), shift(behind, "z", -1)
        pieces += [(step, ahead), (8 - step, behind)]
    ahead, behind = halve(ahead, behind)
    ahead, behind = shift(ahead, "z", 1), shift(behind, "z", -1)
    return pieces + [(4, ahead), (4, behind)]


def close(x):
    return pltpu.with_memory_space_constraint(x, pltpu.VMEM)


def dot(a, b):
    return jnp.dot(a, b, preferred_element_type=F32)


def dot_nt(a, b):
    return lax.dot_general(a, b, NT, preferred_element_type=F32)


def partial_kernel(core_ref, count_ref, hidden_ref, acts_ref, keep_ref, give_ref):
    half, cross = hidden_ref.shape[0] // 2, acts_ref.shape[1] // 2
    core = core_ref[0]
    count = count_ref[0]
    high = lax.broadcasted_iota(jnp.int32, (8, acts_ref.shape[1]), 0) == 0
    counts = jnp.where(high, count // 32, count % 32).astype(F32)
    for mine, ref in ((core, keep_ref), (1 - core, give_ref)):
        hidden = hidden_ref[pl.ds(pl.multiple_of(mine * half, 32), half), :]
        second = acts_ref[1, pl.ds(pl.multiple_of(mine * cross, 32), cross), :]
        ref[pl.ds(0, half), :] = dot_nt(hidden, acts_ref[0]).astype(ref.dtype)
        ref[pl.ds(half, half), :] = dot_nt(hidden, acts_ref[1]).astype(ref.dtype)
        ref[pl.ds(2 * half, cross), :] = dot_nt(second, acts_ref[0]).astype(ref.dtype)
        ref[pl.ds(2 * half + cross, 8), :] = counts.astype(ref.dtype)


def cut_kernel(y_ref, keep_ref, given_ref, hess_ref, hess_give, cross_ref, cross_give):
    rows, quarter = hess_ref.shape[0], cross_ref.shape[0] - 8
    at = pl.multiple_of(rows + y_ref[0] * quarter, 64)
    spots = ((hess_ref, hess_give, 0, 0, rows), (cross_ref, cross_give, 0, at, quarter),
             (cross_ref, cross_give, quarter, rows + 4 * quarter, 8))
    for ref, give, to, start, size in spots:
        total = keep_ref[pl.ds(start, size), :] + given_ref[pl.ds(start, size), :].astype(F32)
        ref[pl.ds(to, size), :] = total
        give[pl.ds(to, size), :] = total.astype(BF16)


def join_cross_kernel(keep_ref, given_ref, out_ref, scale_ref):
    total = keep_ref[...] + given_ref[...].astype(F32)
    rows = out_ref.shape[0]
    scale = 1.0 / (32.0 * total[rows : rows + 1] + total[rows + 1 : rows + 2])
    out_ref[...] = (total[:rows] * scale).astype(BF16)
    scale_ref[...] = jnp.broadcast_to(scale, scale_ref.shape)


def join_kernel(backs, y_ref, keep_ref, given_ref, scale_ref, *refs):
    out_ref, rows = refs[-1], keep_ref.shape[0]
    total = keep_ref[...] + given_ref[...].astype(F32)
    out_ref[pl.ds(0, rows), :] = (total * scale_ref[0:1, :]).astype(BF16)
    for back, ref in zip(backs, refs[:-1]):
        quarter = ref.shape[0]
        at = rows + lax.rem(y_ref[0] + 4 - back, 4) * quarter
        out_ref[pl.ds(pl.multiple_of(at, 64), quarter), :] = ref[...]


def split(x):
    high = x.astype(BF16)
    return high, (x - high.astype(F32)).astype(BF16)


def split_kernel(x_ref, high_ref, low_ref):
    high_ref[...], low_ref[...] = split(x_ref[...])


def stage_kernel(backs, z_ref, *refs):
    pieces, (rows_ref, sems) = refs[: len(backs)], refs[len(backs):]
    depth = pieces[0].shape[1]
    copies = []
    for i, (back, piece) in enumerate(zip(backs, pieces)):
        row = pl.multiple_of(lax.rem(z_ref[0] + 8 - back, 8) * depth, depth)
        for p in range(2):
            to = rows_ref.at[p, pl.ds(row, depth), :]
            copies.append(pltpu.make_async_copy(piece.at[p], to, sems.at[i, p]))
    for copy in copies:
        copy.start()
    for copy in copies:
        copy.wait()


def tail_kernel(
    at_ref, mine_ref, keep_ref, given_ref, high_ref, low_ref, old_ref, _, ahead_ref, behind_ref,
    out_ref, rows_ref, new_buf, sems, new_sems,
):
    zero, z = at_ref[0] == 0, at_ref[1]
    depth, columns = ahead_ref.shape[1:]
    chunks = new_sems.shape[0]
    width = columns // chunks
    row = pl.ds(pl.multiple_of(lax.rem(z + 4, 8) * depth, depth), depth)
    copies = [
        pltpu.make_async_copy(ref.at[0], rows_ref.at[p, row, :], sems.at[p])
        for p, ref in enumerate((ahead_ref, behind_ref))
    ]
    for copy in copies:
        copy.start()

    keep, given = keep_ref[...], given_ref[...]
    low, top = jnp.where(zero, keep, given), jnp.where(zero, given, keep)
    half = old_ref.shape[0] // 2
    first_hess = jnp.concatenate([low[:half], top[:half]], axis=0).astype(F32)
    second_hess = jnp.concatenate([low[half : 2 * half], top[half : 2 * half]], axis=0)
    cross = jnp.concatenate([low[2 * half :], top[2 * half :]], axis=0)
    second = (dot(second_hess, high_ref[1]) + dot(second_hess, low_ref[1])).astype(BF16)
    high, rest = split(first_hess - dot(second, cross))
    first = dot(high, high_ref[0]) + (dot(high, low_ref[0]) + dot(rest, high_ref[0]))
    first = first.astype(BF16)

    index = lax.broadcasted_iota(jnp.int32, (old_ref.shape[0], width), 0)
    gone = index == mine_ref[0]
    for k in range(1, mine_ref.shape[0]):
        gone = gone | (index == mine_ref[k])
    for copy in copies:
        copy.wait()
    outs = []
    for c in range(chunks):
        at = pl.ds(c * width, width)
        change = dot(first, rows_ref[0, :, at]) + dot(second, rows_ref[1, :, at])
        new = jnp.where(gone, 0.0, old_ref[:, at].astype(F32) - change)
        new_buf[:, at] = new.astype(BF16)
        outs.append(pltpu.make_async_copy(new_buf.at[:, at], out_ref.at[:, at], new_sems.at[c]))
        outs[-1].start()
    for copy in outs:
        copy.wait()


def compute(gate_up, counts, panels, inverses, down_weight):
    tokens, _, local = gate_up.shape
    panel = panels.shape[1]
    columns = down_weight.shape[1]
    share = panel // 64
    shard = lax.axis_index("z") * 8 + lax.axis_index("y") * 2 + lax.axis_index("xh")
    core = lax.axis_index("co").astype(jnp.int32)
    mine = lax.dynamic_slice(panels, (0, shard * share), (2, share)).reshape(-1) - shard * local
    onehot = mine[:, None] == jnp.arange(local, dtype=jnp.int32)[None, :]
    select = onehot.astype(BF16)

    slot = jnp.arange(tokens, dtype=jnp.int32)
    valid = (slot < counts[0]).astype(F32)
    gate = gate_up[:, 0, :].astype(F32)
    up = gate_up[:, 1, :].astype(F32)
    hidden = (jax.nn.silu(gate) * up * valid[:, None]).astype(BF16)
    acts = lax.dot_general(select, hidden, NT, preferred_element_type=F32).astype(BF16)
    acts, select = lax.optimization_barrier((acts, select))
    rows = jnp.dot(select, down_weight, preferred_element_type=F32).astype(BF16)

    acts = to_all(acts, "z").reshape(128, tokens)
    near = gather_rows(rows.reshape(2, share, columns))
    acts = spread_acts(acts).reshape(4, 2, 8, 2, share, tokens)
    acts = acts.transpose(3, 2, 0, 1, 4, 5).reshape(2, panel, tokens)
    pieces = ring_z(near)
    inverses, _ = lax.optimization_barrier((inverses, near))
    parts = pl.pallas_call(
        split_kernel,
        out_shape=(jax.ShapeDtypeStruct(inverses.shape, BF16),) * 2,
        in_specs=[VMEM],
        out_specs=(VMEM, VMEM),
        compiler_params=pltpu.CompilerParams(vmem_limit_bytes=12 * 1024 * 1024),
        name="split",
    )(inverses)

    half, cross_half = local // 2, panel // 2
    rows_in_half = 2 * half + cross_half
    keep, give = pl.pallas_call(
        partial_kernel,
        out_shape=(
            jax.ShapeDtypeStruct((rows_in_half + 8, panel), F32),
            jax.ShapeDtypeStruct((rows_in_half + 8, panel), BF16),
        ),
        in_specs=[SMEM, SMEM, VMEM, VMEM],
        out_specs=(VMEM, VMEM),
        compiler_params=pltpu.CompilerParams(vmem_limit_bytes=12 * 1024 * 1024),
        name="partial",
    )(core[None], counts, hidden.T, acts)
    given = shift(give, "co", 1)
    y = lax.axis_index("y").astype(jnp.int32)[None]
    small = pltpu.CompilerParams(vmem_limit_bytes=8 * 1024 * 1024)
    quarter = cross_half // 4
    hess, hess_give, cross, cross_give = pl.pallas_call(
        cut_kernel,
        out_shape=tuple(
            jax.ShapeDtypeStruct((n, panel), d) for n in (2 * half, quarter + 8) for d in (F32, BF16)
        ),
        in_specs=[SMEM, VMEM, VMEM],
        out_specs=(VMEM,) * 4,
        compiler_params=small,
        name="cut",
    )(y, keep, given)
    cross_given = shift(cross_give, "xl", 1)
    hess_given = shift(hess_give, "xl", 1)
    cross, scale = pl.pallas_call(
        join_cross_kernel,
        out_shape=(jax.ShapeDtypeStruct((quarter, panel), BF16), jax.ShapeDtypeStruct((8, panel), F32)),
        in_specs=[VMEM, VMEM],
        out_specs=(VMEM, VMEM),
        compiler_params=small,
        name="join_cross",
    )(cross, cross_given)
    quarters = [(0, cross)] + [(k, shift(cross, "y", k)) for k in (1, 3, 2)]
    keep = pl.pallas_call(
        functools.partial(join_kernel, [k for k, _ in quarters]),
        out_shape=jax.ShapeDtypeStruct((rows_in_half, panel), BF16),
        in_specs=[SMEM] + [VMEM] * 7,
        out_specs=VMEM,
        compiler_params=small,
        name="join",
    )(y, hess, hess_given, scale, *[piece for _, piece in quarters])
    keep = close(keep)
    given = close(shift(keep, "co", 1))

    at = jnp.stack([core, lax.axis_index("z").astype(jnp.int32)])
    staged = pl.pallas_call(
        functools.partial(stage_kernel, [back for back, _ in pieces[:7]]),
        out_shape=jax.ShapeDtypeStruct((2, panel, columns), BF16),
        in_specs=[SMEM] + [ANY] * 7,
        out_specs=VMEM,
        scratch_shapes=[pltpu.SemaphoreType.DMA((7, 2))],
        compiler_params=small,
        name="stage",
    )(at[1:], *[piece for _, piece in pieces[:7]])
    out, _ = pl.pallas_call(
        tail_kernel,
        out_shape=(
            jax.ShapeDtypeStruct((local, columns), BF16),
            jax.ShapeDtypeStruct((2, panel, columns), BF16),
        ),
        in_specs=[SMEM, SMEM] + [VMEM] * 6 + [ANY] * 2,
        out_specs=(HBM, VMEM),
        input_output_aliases={7: 1},
        scratch_shapes=[
            pltpu.VMEM((local, columns), BF16),
            pltpu.SemaphoreType.DMA((2,)),
            pltpu.SemaphoreType.DMA((4,)),
        ],
        compiler_params=pltpu.CompilerParams(vmem_limit_bytes=16 * 1024 * 1024),
        name="tail",
    )(at, mine, keep, given, *parts, down_weight, close(staged), pieces[7][1], pieces[8][1])
    return out


def solution(mesh):
    fine = Mesh(mesh.devices.reshape(8, 4, 2, 2, 2), ("z", "y", "xh", "xl", "co"))
    chan, grp = ("z", "y", "xh"), ("xl", "co")
    in_specs = (P(grp, None, chan), P(grp), P(), P(), P(chan, grp))
    return jax.shard_map(compute, mesh=fine, in_specs=in_specs, out_specs=P(chan, grp), check_vma=False)
```

```python
import functools

import jax
import jax.numpy as jnp
from jax import lax
from jax.experimental import pallas as pl
from jax.experimental.pallas import tpu as pltpu
from jax.sharding import Mesh, PartitionSpec as P


BF16 = jnp.bfloat16
F32 = jnp.float32
NT = (((1,), (1,)), ((), ()))
VMEM = pl.BlockSpec(memory_space=pltpu.VMEM)
SMEM = pl.BlockSpec(memory_space=pltpu.SMEM)
HBM = pl.BlockSpec(memory_space=pltpu.HBM)
ANY = pl.BlockSpec(memory_space=pl.ANY)


def shift(x, axis, by):
    n = lax.axis_size(axis)
    return lax.ppermute(x, axis, [(i, (i + by) % n) for i in range(n)])


def to_all(x, axes):
    n = lax.axis_size(axes)
    return lax.all_to_all(jnp.broadcast_to(x, (n, *x.shape)), axes, split_axis=0, concat_axis=0, tiled=True)


def place(pieces, axis, dim):
    n, me = lax.axis_size(axis), lax.axis_index(axis)
    shape = list(pieces[0][1].shape)
    shape.insert(dim, n)
    out = jnp.zeros(tuple(shape), pieces[0][1].dtype)
    for back, piece in pieces:
        at = [0] * len(shape)
        at[dim] = (me - back) % n
        out = lax.dynamic_update_slice(out, jnp.expand_dims(piece, dim), at)
    return out


def gather_rows(rows, acts):
    other = shift(rows, "xh", 1)
    both = place([(0, rows), (1, other)], "xh", 1)
    others = []
    for k in (1, 3, 2):
        others.append(shift(both, "y", k))
    others, _ = lax.optimization_barrier((others, acts))
    around = place([(0, both)] + list(zip((1, 3, 2), others)), "y", 1)
    return around.reshape(2, 64, rows.shape[-1])


def spread_acts(block):
    other = shift(block, "xh", 1)
    block = place([(0, block), (1, other)], "xh", 0)
    ahead, behind = shift(block, "y", 1), shift(block, "y", -1)
    left, right = shift(ahead[:1], "y", 1), shift(behind[1:], "y", -1)
    far_block = jnp.concatenate([left, right], axis=0)
    return place([(0, block), (1, ahead), (3, behind), (2, far_block)], "y", 0)


def halve_kernel(ahead_ref, behind_ref, first_ref, second_ref, sems):
    copies = [
        pltpu.make_async_copy(ahead_ref.at[pl.ds(0, 1)], first_ref, sems.at[0]),
        pltpu.make_async_copy(behind_ref.at[pl.ds(1, 1)], second_ref, sems.at[1]),
    ]
    for copy in copies:
        copy.start()
    for copy in copies:
        copy.wait()


def halve(ahead, behind):
    half = jax.ShapeDtypeStruct((1, *ahead.shape[1:]), ahead.dtype)
    return pl.pallas_call(
        halve_kernel,
        out_shape=(half, half),
        in_specs=[ANY, ANY],
        out_specs=(ANY, ANY),
        scratch_shapes=[pltpu.SemaphoreType.DMA((2,))],
        compiler_params=pltpu.CompilerParams(vmem_limit_bytes=2 * 1024 * 1024),
        name="halve",
    )(ahead, behind)


def ring_z(block):
    pieces = [(0, block)]
    ahead, behind = block, block
    for step in (1, 2, 3):
        ahead, behind = shift(ahead, "z", 1), shift(behind, "z", -1)
        pieces += [(step, ahead), (8 - step, behind)]
    ahead, behind = halve(ahead, behind)
    ahead, behind = shift(ahead, "z", 1), shift(behind, "z", -1)
    return pieces + [(4, ahead), (4, behind)]


def close(x):
    return pltpu.with_memory_space_constraint(x, pltpu.VMEM)


def dot(a, b):
    return jnp.dot(a, b, preferred_element_type=F32)


def dot_nt(a, b):
    return lax.dot_general(a, b, NT, preferred_element_type=F32)


def partial_kernel(core_ref, count_ref, hidden_ref, acts_ref, keep_ref, give_ref):
    half, cross = hidden_ref.shape[0] // 2, acts_ref.shape[1] // 2
    core = core_ref[0]
    count = count_ref[0]
    high = lax.broadcasted_iota(jnp.int32, (8, acts_ref.shape[1]), 0) == 0
    counts = jnp.where(high, count // 32, count % 32).astype(F32)
    for mine, ref in ((core, keep_ref), (1 - core, give_ref)):
        hidden = hidden_ref[pl.ds(pl.multiple_of(mine * half, 32), half), :]
        second = acts_ref[1, pl.ds(pl.multiple_of(mine * cross, 32), cross), :]
        ref[pl.ds(0, half), :] = dot_nt(hidden, acts_ref[0]).astype(ref.dtype)
        ref[pl.ds(half, half), :] = dot_nt(hidden, acts_ref[1]).astype(ref.dtype)
        ref[pl.ds(2 * half, cross), :] = dot_nt(second, acts_ref[0]).astype(ref.dtype)
        ref[pl.ds(2 * half + cross, 8), :] = counts.astype(ref.dtype)


def cut_kernel(y_ref, keep_ref, given_ref, hess_ref, hess_give, cross_ref, cross_give):
    rows, quarter = hess_ref.shape[0], cross_ref.shape[0] - 8
    at = pl.multiple_of(rows + y_ref[0] * quarter, 64)
    spots = ((hess_ref, hess_give, 0, 0, rows), (cross_ref, cross_give, 0, at, quarter),
             (cross_ref, cross_give, quarter, rows + 4 * quarter, 8))
    for ref, give, to, start, size in spots:
        total = keep_ref[pl.ds(start, size), :] + given_ref[pl.ds(start, size), :].astype(F32)
        ref[pl.ds(to, size), :] = total
        give[pl.ds(to, size), :] = total.astype(BF16)


def join_cross_kernel(keep_ref, given_ref, out_ref, scale_ref):
    total = keep_ref[...] + given_ref[...].astype(F32)
    rows = out_ref.shape[0]
    scale = 1.0 / (32.0 * total[rows : rows + 1] + total[rows + 1 : rows + 2])
    out_ref[...] = (total[:rows] * scale).astype(BF16)
    scale_ref[...] = jnp.broadcast_to(scale, scale_ref.shape)


def join_kernel(backs, y_ref, keep_ref, given_ref, scale_ref, *refs):
    out_ref, rows = refs[-1], keep_ref.shape[0]
    total = keep_ref[...] + given_ref[...].astype(F32)
    out_ref[pl.ds(0, rows), :] = (total * scale_ref[0:1, :]).astype(BF16)
    for back, ref in zip(backs, refs[:-1]):
        quarter = ref.shape[0]
        at = rows + lax.rem(y_ref[0] + 4 - back, 4) * quarter
        out_ref[pl.ds(pl.multiple_of(at, 64), quarter), :] = ref[...]


def split(x):
    high = x.astype(BF16)
    return high, (x - high.astype(F32)).astype(BF16)


def split_kernel(x_ref, high_ref, low_ref):
    high_ref[...], low_ref[...] = split(x_ref[...])


def stage_kernel(backs, z_ref, *refs):
    pieces, (rows_ref, sems) = refs[: len(backs)], refs[len(backs):]
    depth = pieces[0].shape[1]
    copies = []
    for i, (back, piece) in enumerate(zip(backs, pieces)):
        row = pl.multiple_of(lax.rem(z_ref[0] + 8 - back, 8) * depth, depth)
        for p in range(2):
            to = rows_ref.at[p, pl.ds(row, depth), :]
            copies.append(pltpu.make_async_copy(piece.at[p], to, sems.at[i, p]))
    for copy in copies:
        copy.start()
    for copy in copies:
        copy.wait()


def tail_kernel(
    at_ref, mine_ref, keep_ref, given_ref, high_ref, low_ref, old_ref, _, ahead_ref, behind_ref,
    out_ref, rows_ref, new_buf, sems, new_sems,
):
    zero, z = at_ref[0] == 0, at_ref[1]
    depth, columns = ahead_ref.shape[1:]
    chunks = new_sems.shape[0]
    width = columns // chunks
    row = pl.ds(pl.multiple_of(lax.rem(z + 4, 8) * depth, depth), depth)
    copies = [
        pltpu.make_async_copy(ref.at[0], rows_ref.at[p, row, :], sems.at[p])
        for p, ref in enumerate((ahead_ref, behind_ref))
    ]
    for copy in copies:
        copy.start()

    keep, given = keep_ref[...], given_ref[...]
    low, top = jnp.where(zero, keep, given), jnp.where(zero, given, keep)
    half = old_ref.shape[0] // 2
    first_hess = jnp.concatenate([low[:half], top[:half]], axis=0).astype(F32)
    second_hess = jnp.concatenate([low[half : 2 * half], top[half : 2 * half]], axis=0)
    cross = jnp.concatenate([low[2 * half :], top[2 * half :]], axis=0)
    second = (dot(second_hess, high_ref[1]) + dot(second_hess, low_ref[1])).astype(BF16)
    high, rest = split(first_hess - dot(second, cross))
    first = dot(high, high_ref[0]) + (dot(high, low_ref[0]) + dot(rest, high_ref[0]))
    first = first.astype(BF16)

    index = lax.broadcasted_iota(jnp.int32, (old_ref.shape[0], width), 0)
    gone = index == mine_ref[0]
    for k in range(1, mine_ref.shape[0]):
        gone = gone | (index == mine_ref[k])
    for copy in copies:
        copy.wait()
    outs = []
    for c in range(chunks):
        at = pl.ds(c * width, width)
        change = dot(first, rows_ref[0, :, at]) + dot(second, rows_ref[1, :, at])
        new = jnp.where(gone, 0.0, old_ref[:, at].astype(F32) - change)
        new_buf[:, at] = new.astype(BF16)
        outs.append(pltpu.make_async_copy(new_buf.at[:, at], out_ref.at[:, at], new_sems.at[c]))
        outs[-1].start()
    for copy in outs:
        copy.wait()


def compute(gate_up, counts, panels, inverses, down_weight):
    tokens, _, local = gate_up.shape
    panel = panels.shape[1]
    columns = down_weight.shape[1]
    share = panel // 64
    shard = lax.axis_index("z") * 8 + lax.axis_index("y") * 2 + lax.axis_index("xh")
    core = lax.axis_index("co").astype(jnp.int32)
    mine = lax.dynamic_slice(panels, (0, shard * share), (2, share)).reshape(-1) - shard * local
    onehot = mine[:, None] == jnp.arange(local, dtype=jnp.int32)[None, :]
    select = onehot.astype(BF16)

    slot = jnp.arange(tokens, dtype=jnp.int32)
    valid = (slot < counts[0]).astype(F32)
    gate = gate_up[:, 0, :].astype(F32)
    up = gate_up[:, 1, :].astype(F32)
    hidden = (jax.nn.silu(gate) * up * valid[:, None]).astype(BF16)
    acts = lax.dot_general(select, hidden, NT, preferred_element_type=F32).astype(BF16)
    acts, select = lax.optimization_barrier((acts, select))
    rows = jnp.dot(select, down_weight, preferred_element_type=F32).astype(BF16)

    acts = to_all(acts, "z").reshape(128, tokens)
    near = gather_rows(rows.reshape(2, share, columns), acts)
    acts = spread_acts(acts).reshape(4, 2, 8, 2, share, tokens)
    acts = acts.transpose(3, 2, 0, 1, 4, 5).reshape(2, panel, tokens)
    pieces = ring_z(near)
    inverses, _ = lax.optimization_barrier((inverses, near))
    parts = pl.pallas_call(
        split_kernel,
        out_shape=(jax.ShapeDtypeStruct(inverses.shape, BF16),) * 2,
        in_specs=[VMEM],
        out_specs=(VMEM, VMEM),
        compiler_params=pltpu.CompilerParams(vmem_limit_bytes=12 * 1024 * 1024),
        name="split",
    )(inverses)

    half, cross_half = local // 2, panel // 2
    rows_in_half = 2 * half + cross_half
    keep, give = pl.pallas_call(
        partial_kernel,
        out_shape=(
            jax.ShapeDtypeStruct((rows_in_half + 8, panel), F32),
            jax.ShapeDtypeStruct((rows_in_half + 8, panel), BF16),
        ),
        in_specs=[SMEM, SMEM, VMEM, VMEM],
        out_specs=(VMEM, VMEM),
        compiler_params=pltpu.CompilerParams(vmem_limit_bytes=12 * 1024 * 1024),
        name="partial",
    )(core[None], counts, hidden.T, acts)
    given = shift(give, "co", 1)
    y = lax.axis_index("y").astype(jnp.int32)[None]
    small = pltpu.CompilerParams(vmem_limit_bytes=8 * 1024 * 1024)
    quarter = cross_half // 4
    hess, hess_give, cross, cross_give = pl.pallas_call(
        cut_kernel,
        out_shape=tuple(
            jax.ShapeDtypeStruct((n, panel), d) for n in (2 * half, quarter + 8) for d in (F32, BF16)
        ),
        in_specs=[SMEM, VMEM, VMEM],
        out_specs=(VMEM,) * 4,
        compiler_params=small,
        name="cut",
    )(y, keep, given)
    cross_given = shift(cross_give, "xl", 1)
    hess_given = shift(hess_give, "xl", 1)
    cross, scale = pl.pallas_call(
        join_cross_kernel,
        out_shape=(jax.ShapeDtypeStruct((quarter, panel), BF16), jax.ShapeDtypeStruct((8, panel), F32)),
        in_specs=[VMEM, VMEM],
        out_specs=(VMEM, VMEM),
        compiler_params=small,
        name="join_cross",
    )(cross, cross_given)
    quarters = [(0, cross)] + [(k, shift(cross, "y", k)) for k in (1, 3, 2)]
    keep = pl.pallas_call(
        functools.partial(join_kernel, [k for k, _ in quarters]),
        out_shape=jax.ShapeDtypeStruct((rows_in_half, panel), BF16),
        in_specs=[SMEM] + [VMEM] * 7,
        out_specs=VMEM,
        compiler_params=small,
        name="join",
    )(y, hess, hess_given, scale, *[piece for _, piece in quarters])
    keep = close(keep)
    given = close(shift(keep, "co", 1))

    at = jnp.stack([core, lax.axis_index("z").astype(jnp.int32)])
    staged = pl.pallas_call(
        functools.partial(stage_kernel, [back for back, _ in pieces[:7]]),
        out_shape=jax.ShapeDtypeStruct((2, panel, columns), BF16),
        in_specs=[SMEM] + [ANY] * 7,
        out_specs=VMEM,
        scratch_shapes=[pltpu.SemaphoreType.DMA((7, 2))],
        compiler_params=small,
        name="stage",
    )(at[1:], *[piece for _, piece in pieces[:7]])
    out, _ = pl.pallas_call(
        tail_kernel,
        out_shape=(
            jax.ShapeDtypeStruct((local, columns), BF16),
            jax.ShapeDtypeStruct((2, panel, columns), BF16),
        ),
        in_specs=[SMEM, SMEM] + [VMEM] * 6 + [ANY] * 2,
        out_specs=(HBM, VMEM),
        input_output_aliases={7: 1},
        scratch_shapes=[
            pltpu.VMEM((local, columns), BF16),
            pltpu.SemaphoreType.DMA((2,)),
            pltpu.SemaphoreType.DMA((4,)),
        ],
        compiler_params=pltpu.CompilerParams(vmem_limit_bytes=16 * 1024 * 1024),
        name="tail",
    )(at, mine, keep, given, *parts, down_weight, close(staged), pieces[7][1], pieces[8][1])
    return out


def solution(mesh):
    fine = Mesh(mesh.devices.reshape(8, 4, 2, 2, 2), ("z", "y", "xh", "xl", "co"))
    chan, grp = ("z", "y", "xh"), ("xl", "co")
    in_specs = (P(grp, None, chan), P(grp), P(), P(), P(chan, grp))
    return jax.shard_map(compute, mesh=fine, in_specs=in_specs, out_specs=P(chan, grp), check_vma=False)
```

```python
import functools

import jax
import jax.numpy as jnp
from jax import lax
from jax.experimental import pallas as pl
from jax.experimental.pallas import tpu as pltpu
from jax.sharding import Mesh, PartitionSpec as P


BF16 = jnp.bfloat16
F32 = jnp.float32
NT = (((1,), (1,)), ((), ()))
VMEM = pl.BlockSpec(memory_space=pltpu.VMEM)
SMEM = pl.BlockSpec(memory_space=pltpu.SMEM)
HBM = pl.BlockSpec(memory_space=pltpu.HBM)
ANY = pl.BlockSpec(memory_space=pl.ANY)


def shift(x, axis, by):
    n = lax.axis_size(axis)
    return lax.ppermute(x, axis, [(i, (i + by) % n) for i in range(n)])


def to_all(x, axes):
    n = lax.axis_size(axes)
    return lax.all_to_all(jnp.broadcast_to(x, (n, *x.shape)), axes, split_axis=0, concat_axis=0, tiled=True)


def place(pieces, axis, dim):
    n, me = lax.axis_size(axis), lax.axis_index(axis)
    shape = list(pieces[0][1].shape)
    shape.insert(dim, n)
    out = jnp.zeros(tuple(shape), pieces[0][1].dtype)
    for back, piece in pieces:
        at = [0] * len(shape)
        at[dim] = (me - back) % n
        out = lax.dynamic_update_slice(out, jnp.expand_dims(piece, dim), at)
    return out


def gather_rows(rows, acts):
    other = shift(rows, "xh", 1)
    both = place([(0, rows), (1, other)], "xh", 1)
    others = []
    for k in (1, 3, 2):
        others.append(shift(both, "y", k))
    others, _ = lax.optimization_barrier((others, acts))
    around = place([(0, both)] + list(zip((1, 3, 2), others)), "y", 1)
    return around.reshape(2, 64, rows.shape[-1])


def spread_acts(block):
    half = block.shape[1] // 2
    one, two = block[:, :half], block[:, half:]
    other = shift(one, "xh", 1)
    others = [(k, shift(two, "y", k)) for k in (1, 3, 2)]
    one = place([(0, one), (1, other)], "xh", 0)
    ahead, behind = shift(one, "y", 1), shift(one, "y", -1)
    two = place([(0, two)] + others, "y", 0)
    other = shift(two, "xh", 1)
    left, right = shift(ahead[:1], "y", 1), shift(behind[1:], "y", -1)
    far_block = jnp.concatenate([left, right], axis=0)
    one = place([(0, one), (1, ahead), (3, behind), (2, far_block)], "y", 0)
    two = place([(0, two), (1, other)], "xh", 1)
    return jnp.concatenate([one, two], axis=-1)


def halve_kernel(ahead_ref, behind_ref, first_ref, second_ref, sems):
    copies = [
        pltpu.make_async_copy(ahead_ref.at[pl.ds(0, 1)], first_ref, sems.at[0]),
        pltpu.make_async_copy(behind_ref.at[pl.ds(1, 1)], second_ref, sems.at[1]),
    ]
    for copy in copies:
        copy.start()
    for copy in copies:
        copy.wait()


def halve(ahead, behind):
    half = jax.ShapeDtypeStruct((1, *ahead.shape[1:]), ahead.dtype)
    return pl.pallas_call(
        halve_kernel,
        out_shape=(half, half),
        in_specs=[ANY, ANY],
        out_specs=(ANY, ANY),
        scratch_shapes=[pltpu.SemaphoreType.DMA((2,))],
        compiler_params=pltpu.CompilerParams(vmem_limit_bytes=2 * 1024 * 1024),
        name="halve",
    )(ahead, behind)


def ring_z(block):
    pieces = [(0, block)]
    ahead, behind = block, block
    for step in (1, 2, 3):
        ahead, behind = shift(ahead, "z", 1), shift(behind, "z", -1)
        pieces += [(step, ahead), (8 - step, behind)]
    ahead, behind = halve(ahead, behind)
    ahead, behind = shift(ahead, "z", 1), shift(behind, "z", -1)
    return pieces + [(4, ahead), (4, behind)]


def close(x):
    return pltpu.with_memory_space_constraint(x, pltpu.VMEM)


def dot(a, b):
    return jnp.dot(a, b, preferred_element_type=F32)


def dot_nt(a, b):
    return lax.dot_general(a, b, NT, preferred_element_type=F32)


def partial_kernel(core_ref, count_ref, hidden_ref, acts_ref, keep_ref, give_ref):
    half, cross = hidden_ref.shape[0] // 2, acts_ref.shape[1] // 2
    core = core_ref[0]
    count = count_ref[0]
    high = lax.broadcasted_iota(jnp.int32, (8, acts_ref.shape[1]), 0) == 0
    counts = jnp.where(high, count // 32, count % 32).astype(F32)
    for mine, ref in ((core, keep_ref), (1 - core, give_ref)):
        hidden = hidden_ref[pl.ds(pl.multiple_of(mine * half, 32), half), :]
        second = acts_ref[1, pl.ds(pl.multiple_of(mine * cross, 32), cross), :]
        ref[pl.ds(0, half), :] = dot_nt(hidden, acts_ref[0]).astype(ref.dtype)
        ref[pl.ds(half, half), :] = dot_nt(hidden, acts_ref[1]).astype(ref.dtype)
        ref[pl.ds(2 * half, cross), :] = dot_nt(second, acts_ref[0]).astype(ref.dtype)
        ref[pl.ds(2 * half + cross, 8), :] = counts.astype(ref.dtype)


def cut_kernel(y_ref, keep_ref, given_ref, hess_ref, hess_give, cross_ref, cross_give):
    rows, quarter = hess_ref.shape[0], cross_ref.shape[0] - 8
    at = pl.multiple_of(rows + y_ref[0] * quarter, 64)
    spots = ((hess_ref, hess_give, 0, 0, rows), (cross_ref, cross_give, 0, at, quarter),
             (cross_ref, cross_give, quarter, rows + 4 * quarter, 8))
    for ref, give, to, start, size in spots:
        total = keep_ref[pl.ds(start, size), :] + given_ref[pl.ds(start, size), :].astype(F32)
        ref[pl.ds(to, size), :] = total
        give[pl.ds(to, size), :] = total.astype(BF16)


def join_cross_kernel(keep_ref, given_ref, out_ref, scale_ref):
    total = keep_ref[...] + given_ref[...].astype(F32)
    rows = out_ref.shape[0]
    scale = 1.0 / (32.0 * total[rows : rows + 1] + total[rows + 1 : rows + 2])
    out_ref[...] = (total[:rows] * scale).astype(BF16)
    scale_ref[...] = jnp.broadcast_to(scale, scale_ref.shape)


def join_kernel(backs, y_ref, keep_ref, given_ref, scale_ref, *refs):
    out_ref, rows = refs[-1], keep_ref.shape[0]
    total = keep_ref[...] + given_ref[...].astype(F32)
    out_ref[pl.ds(0, rows), :] = (total * scale_ref[0:1, :]).astype(BF16)
    for back, ref in zip(backs, refs[:-1]):
        quarter = ref.shape[0]
        at = rows + lax.rem(y_ref[0] + 4 - back, 4) * quarter
        out_ref[pl.ds(pl.multiple_of(at, 64), quarter), :] = ref[...]


def split(x):
    high = x.astype(BF16)
    return high, (x - high.astype(F32)).astype(BF16)


def split_kernel(x_ref, high_ref, low_ref):
    high_ref[...], low_ref[...] = split(x_ref[...])


def stage_kernel(backs, z_ref, *refs):
    pieces, (rows_ref, sems) = refs[: len(backs)], refs[len(backs):]
    depth = pieces[0].shape[1]
    copies = []
    for i, (back, piece) in enumerate(zip(backs, pieces)):
        row = pl.multiple_of(lax.rem(z_ref[0] + 8 - back, 8) * depth, depth)
        for p in range(2):
            to = rows_ref.at[p, pl.ds(row, depth), :]
            copies.append(pltpu.make_async_copy(piece.at[p], to, sems.at[i, p]))
    for copy in copies:
        copy.start()
    for copy in copies:
        copy.wait()


def tail_kernel(
    at_ref, mine_ref, keep_ref, given_ref, high_ref, low_ref, old_ref, _, ahead_ref, behind_ref,
    out_ref, rows_ref, new_buf, sems, new_sems,
):
    zero, z = at_ref[0] == 0, at_ref[1]
    depth, columns = ahead_ref.shape[1:]
    chunks = new_sems.shape[0]
    width = columns // chunks
    row = pl.ds(pl.multiple_of(lax.rem(z + 4, 8) * depth, depth), depth)
    copies = [
        pltpu.make_async_copy(ref.at[0], rows_ref.at[p, row, :], sems.at[p])
        for p, ref in enumerate((ahead_ref, behind_ref))
    ]
    for copy in copies:
        copy.start()

    keep, given = keep_ref[...], given_ref[...]
    low, top = jnp.where(zero, keep, given), jnp.where(zero, given, keep)
    half = old_ref.shape[0] // 2
    first_hess = jnp.concatenate([low[:half], top[:half]], axis=0).astype(F32)
    second_hess = jnp.concatenate([low[half : 2 * half], top[half : 2 * half]], axis=0)
    cross = jnp.concatenate([low[2 * half :], top[2 * half :]], axis=0)
    second = (dot(second_hess, high_ref[1]) + dot(second_hess, low_ref[1])).astype(BF16)
    high, rest = split(first_hess - dot(second, cross))
    first = dot(high, high_ref[0]) + (dot(high, low_ref[0]) + dot(rest, high_ref[0]))
    first = first.astype(BF16)

    index = lax.broadcasted_iota(jnp.int32, (old_ref.shape[0], width), 0)
    gone = index == mine_ref[0]
    for k in range(1, mine_ref.shape[0]):
        gone = gone | (index == mine_ref[k])
    for copy in copies:
        copy.wait()
    outs = []
    for c in range(chunks):
        at = pl.ds(c * width, width)
        change = dot(first, rows_ref[0, :, at]) + dot(second, rows_ref[1, :, at])
        new = jnp.where(gone, 0.0, old_ref[:, at].astype(F32) - change)
        new_buf[:, at] = new.astype(BF16)
        outs.append(pltpu.make_async_copy(new_buf.at[:, at], out_ref.at[:, at], new_sems.at[c]))
        outs[-1].start()
    for copy in outs:
        copy.wait()


def compute(gate_up, counts, panels, inverses, down_weight):
    tokens, _, local = gate_up.shape
    panel = panels.shape[1]
    columns = down_weight.shape[1]
    share = panel // 64
    shard = lax.axis_index("z") * 8 + lax.axis_index("y") * 2 + lax.axis_index("xh")
    core = lax.axis_index("co").astype(jnp.int32)
    mine = lax.dynamic_slice(panels, (0, shard * share), (2, share)).reshape(-1) - shard * local
    onehot = mine[:, None] == jnp.arange(local, dtype=jnp.int32)[None, :]
    select = onehot.astype(BF16)

    slot = jnp.arange(tokens, dtype=jnp.int32)
    valid = (slot < counts[0]).astype(F32)
    gate = gate_up[:, 0, :].astype(F32)
    up = gate_up[:, 1, :].astype(F32)
    hidden = (jax.nn.silu(gate) * up * valid[:, None]).astype(BF16)
    acts = lax.dot_general(select, hidden, NT, preferred_element_type=F32).astype(BF16)
    acts, select = lax.optimization_barrier((acts, select))
    rows = jnp.dot(select, down_weight, preferred_element_type=F32).astype(BF16)

    acts = to_all(acts, "z").reshape(128, tokens)
    near = gather_rows(rows.reshape(2, share, columns), acts)
    acts = spread_acts(acts).reshape(4, 2, 8, 2, share, tokens)
    acts = acts.transpose(3, 2, 0, 1, 4, 5).reshape(2, panel, tokens)
    pieces = ring_z(near)
    inverses, _ = lax.optimization_barrier((inverses, near))
    parts = pl.pallas_call(
        split_kernel,
        out_shape=(jax.ShapeDtypeStruct(inverses.shape, BF16),) * 2,
        in_specs=[VMEM],
        out_specs=(VMEM, VMEM),
        compiler_params=pltpu.CompilerParams(vmem_limit_bytes=12 * 1024 * 1024),
        name="split",
    )(inverses)

    half, cross_half = local // 2, panel // 2
    rows_in_half = 2 * half + cross_half
    keep, give = pl.pallas_call(
        partial_kernel,
        out_shape=(
            jax.ShapeDtypeStruct((rows_in_half + 8, panel), F32),
            jax.ShapeDtypeStruct((rows_in_half + 8, panel), BF16),
        ),
        in_specs=[SMEM, SMEM, VMEM, VMEM],
        out_specs=(VMEM, VMEM),
        compiler_params=pltpu.CompilerParams(vmem_limit_bytes=12 * 1024 * 1024),
        name="partial",
    )(core[None], counts, hidden.T, acts)
    given = shift(give, "co", 1)
    y = lax.axis_index("y").astype(jnp.int32)[None]
    small = pltpu.CompilerParams(vmem_limit_bytes=8 * 1024 * 1024)
    quarter = cross_half // 4
    hess, hess_give, cross, cross_give = pl.pallas_call(
        cut_kernel,
        out_shape=tuple(
            jax.ShapeDtypeStruct((n, panel), d) for n in (2 * half, quarter + 8) for d in (F32, BF16)
        ),
        in_specs=[SMEM, VMEM, VMEM],
        out_specs=(VMEM,) * 4,
        compiler_params=small,
        name="cut",
    )(y, keep, given)
    cross_given = shift(cross_give, "xl", 1)
    hess_given = shift(hess_give, "xl", 1)
    cross, scale = pl.pallas_call(
        join_cross_kernel,
        out_shape=(jax.ShapeDtypeStruct((quarter, panel), BF16), jax.ShapeDtypeStruct((8, panel), F32)),
        in_specs=[VMEM, VMEM],
        out_specs=(VMEM, VMEM),
        compiler_params=small,
        name="join_cross",
    )(cross, cross_given)
    quarters = [(0, cross)] + [(k, shift(cross, "y", k)) for k in (1, 3, 2)]
    keep = pl.pallas_call(
        functools.partial(join_kernel, [k for k, _ in quarters]),
        out_shape=jax.ShapeDtypeStruct((rows_in_half, panel), BF16),
        in_specs=[SMEM] + [VMEM] * 7,
        out_specs=VMEM,
        compiler_params=small,
        name="join",
    )(y, hess, hess_given, scale, *[piece for _, piece in quarters])
    keep = close(keep)
    given = close(shift(keep, "co", 1))

    at = jnp.stack([core, lax.axis_index("z").astype(jnp.int32)])
    staged = pl.pallas_call(
        functools.partial(stage_kernel, [back for back, _ in pieces[:7]]),
        out_shape=jax.ShapeDtypeStruct((2, panel, columns), BF16),
        in_specs=[SMEM] + [ANY] * 7,
        out_specs=VMEM,
        scratch_shapes=[pltpu.SemaphoreType.DMA((7, 2))],
        compiler_params=small,
        name="stage",
    )(at[1:], *[piece for _, piece in pieces[:7]])
    out, _ = pl.pallas_call(
        tail_kernel,
        out_shape=(
            jax.ShapeDtypeStruct((local, columns), BF16),
            jax.ShapeDtypeStruct((2, panel, columns), BF16),
        ),
        in_specs=[SMEM, SMEM] + [VMEM] * 6 + [ANY] * 2,
        out_specs=(HBM, VMEM),
        input_output_aliases={7: 1},
        scratch_shapes=[
            pltpu.VMEM((local, columns), BF16),
            pltpu.SemaphoreType.DMA((2,)),
            pltpu.SemaphoreType.DMA((4,)),
        ],
        compiler_params=pltpu.CompilerParams(vmem_limit_bytes=16 * 1024 * 1024),
        name="tail",
    )(at, mine, keep, given, *parts, down_weight, close(staged), pieces[7][1], pieces[8][1])
    return out


def solution(mesh):
    fine = Mesh(mesh.devices.reshape(8, 4, 2, 2, 2), ("z", "y", "xh", "xl", "co"))
    chan, grp = ("z", "y", "xh"), ("xl", "co")
    in_specs = (P(grp, None, chan), P(grp), P(), P(), P(chan, grp))
    return jax.shard_map(compute, mesh=fine, in_specs=in_specs, out_specs=P(chan, grp), check_vma=False)
```
